256 devices in a mesh: box: 128 (over z, x, y), help: 2 (over core).
Axes of the slice: x: 4, y: 4, z: 8, core: 2. Of those that a mesh axis runs over, the one named last changes fastest.
Arguments:
- prim_pos: float32 [3, 16384], P(None, ('box', 'help')), may hold values from 0 to 1
- prim_weight: float32 [16384], P(('box', 'help')), may hold values from 0.3 to 3
- sec_pos: float32 [2048, 3, 128], P(('box', 'help')), may hold values from 0 to 1
- sec_weight: float32 [2048, 128], P(('box', 'help')), may hold values from 0.3 to 3
- sec_counts: int32 [2048], P(('box', 'help')), may hold values from 1 to 128, as said below
- tile_lists: int32 [1024, 12], P(('box', 'help')), may hold values from -1 to 2047, as said below
- region_of: int32 [16384, 1], P(('box', 'help')), may hold values from 0 to 255; in each aligned block of 64 rows (0 to 63, 64 to 127, ...) at most 2 rows name the same one
Outputs:
- coefficients: bfloat16 [16384, 1936], P(('box', 'help'))
- region_tensor: float32 [256, 129536], P(('box', 'help'))
The draws below stay inside these ranges and needn't reach their ends.
Inputs may be any that keep to these rules, and one draw needn't show every extreme that they name: Block g holds sec_counts[g] live secondaries in its first slots; every device holds at least one block with all 128 slots live. `tile_lists`: row t lists distinct blocks for the primaries t * 16 to (t + 1) * 16 - 1. Every listed block belongs to a device whose box index is within one, cyclically, of the box index of the device that holds the tile, with any help index. Unused slots hold -1 and come after the used ones; at least 6 slots are used, and each device has a tile that uses all 12. `region_of`: within the rows of one device (aligned blocks of 64 rows) no region is named more than 2 times, a bound that some block reaches. Region r is owned by the device of index r along box+help.
All inputs are finite; a program needn't handle non-finite values.
Results may differ from the reference program's by a relative error of at most 0.0075.
Values may be sent and summed in bfloat16 or wider, within the bound.
A program may use at most 64 MiB of HBM per device.

```python
import math
import jax
import jax.numpy as jnp
import numpy as np
from jax import lax

LMAX = 10
NBIN = 16
BS = 128
LIST = 12
PT = 16
BLK_DEV = 8
PRIM_DEV = 64
FEAT = 1936
TOTAL = 129536
REGIONS = 256
CAP = 2
NPRIM = 16384
NBLK = 2048
N_BOX = 128
N_HELP = 2


def draw_sec_counts(key, part):
    drawn_count = jax.random.randint(jax.random.fold_in(key, 3), (NBLK,), 1, BS + 1, dtype=jnp.int32)
    full_slot = jax.random.randint(jax.random.fold_in(key, 4), (NBLK // BLK_DEV,), 0, BLK_DEV, dtype=jnp.int32)
    block_index = jnp.arange(NBLK, dtype=jnp.int32)
    full_block = block_index % BLK_DEV == jnp.repeat(full_slot, BLK_DEV)
    return jnp.where(full_block, BS, drawn_count).astype(jnp.int32)


def draw_tile_lists(key, part):
    tile_count = NPRIM // PT
    tiles_device = PRIM_DEV // PT
    pool_size = 6 * BLK_DEV
    tile_keys = jax.random.split(jax.random.fold_in(key, 11), tile_count)
    pool_picks = jax.vmap(lambda tile_key: jax.random.permutation(tile_key, pool_size)[:LIST])(tile_keys).astype(jnp.int32)
    tile_index = jnp.arange(tile_count, dtype=jnp.int32)
    device_index = tile_index // tiles_device
    box_of_tile = device_index // N_HELP
    box_move = pool_picks // (N_HELP * BLK_DEV) - 1
    helper = pool_picks // BLK_DEV % N_HELP
    local_slot = pool_picks % BLK_DEV
    target_box = jnp.mod(box_of_tile[:, None] + box_move, N_BOX)
    listed = (target_box * N_HELP + helper) * BLK_DEV + local_slot
    length = jax.random.randint(jax.random.fold_in(key, 12), (tile_count,), LIST // 2, LIST + 1, dtype=jnp.int32)
    full_tile = jax.random.randint(jax.random.fold_in(key, 13), (NPRIM // PRIM_DEV,), 0, tiles_device, dtype=jnp.int32)
    length = jnp.where(tile_index % tiles_device == full_tile[device_index], LIST, length)
    slot_index = jnp.arange(LIST, dtype=jnp.int32)
    return jnp.where(slot_index[None, :] < length[:, None], listed, -1).astype(jnp.int32)


def block_levels(rng, extent, cuts, low, largest):
    factor_of, own = 1.0, jax.random.fold_in(rng, 6)
    for axis_at, blocks in cuts:
        steps = jnp.exp(jax.random.uniform(jax.random.fold_in(own, axis_at), (blocks,), jnp.float32, low / len(cuts), largest / len(cuts)))
        factor_of = factor_of * jnp.repeat(steps, extent[axis_at] // blocks).reshape([-1 if axis == axis_at else 1 for axis in range(len(extent))])
    return factor_of


def deal_out(key, own, number, rows, amount, top, most, slope):
    order = jax.random.permutation(key, amount)
    crowded, common = load_shares(amount, rows * top, most, slope, True), load_shares(amount, rows * top, most, slope, False)
    places = jnp.arange(amount)

    def named(tallies, offset_by):
        used = int((tallies > 0).sum())
        fixed = max(1, used // 4)
        moved = fixed + (places - fixed + offset_by * (used - fixed)) % max(1, amount - fixed)
        return jnp.zeros((amount,), jnp.int32).at[order[jnp.where(places < fixed, places, moved)]].set(jnp.asarray(tallies, jnp.int32))

    tallies = jnp.where(number % 4 == 0, named(crowded, number // 4), named(common, number - number // 4 - 1))
    mixed = jax.random.permutation(jax.random.fold_in(own, 3), amount)
    giver, taker = mixed[0:amount // 2 * 2:2], mixed[1:amount // 2 * 2:2]
    margin = jnp.minimum(tallies[giver] - 1, most - tallies[taker]) // 2
    margin = jnp.where((giver == order[0]) | (taker == order[0]) | (tallies[taker] == 0), 0, jnp.maximum(margin, 0))
    moved = jax.random.randint(jax.random.fold_in(own, 4), (amount // 2,), 0, 1 << 20) % (margin + 1)
    tallies = tallies.at[giver].add(-moved).at[taker].add(moved)
    labels = jnp.searchsorted(jnp.cumsum(tallies), jnp.arange(rows * top), side="right").astype(jnp.int32)
    listing = labels.reshape(top, rows).T
    listing = listing[jax.random.permutation(jax.random.fold_in(own, 1), rows)]
    offset_by = jax.random.randint(jax.random.fold_in(own, 2), (rows, 1), 0, top)
    return jnp.take_along_axis(listing, (jnp.arange(top)[None, :] + offset_by) % top, axis=1)


def load_shares(count, total, reach, lean, full):
    weights = [(1 << 20) // math.isqrt(rank ** lean) + 1 for rank in range(1, count + 1)]
    largest = reach if full else min(reach, max(-(-total // count), total * weights[0] // sum(weights)))
    least = 1 if total - largest >= count - 1 else 0
    given, surplus = [largest] + [least] * (count - 1), total - largest - least * (count - 1)
    while surplus > 0:
        movable = [i for i in range(1, count) if given[i] < largest] or [i for i in range(1, count) if given[i] < reach]
        pool, remaining = sum([weights[i] for i in movable]), surplus
        for i in movable:
            addition = min(reach - given[i], max(1, remaining * weights[i] // pool), surplus)
            given[i] = given[i] + addition
            surplus = surplus - addition
    return np.array(given)


def setup_inputs(seed: int = 0) -> dict:
    arg_keys = jax.random.split(jax.random.key(seed), 8)
    prim_pos = jnp.clip(1.0 * jax.random.uniform(arg_keys[0], (3, NPRIM), jnp.float32) ** block_levels(arg_keys[0], (3, NPRIM), ((1, 256),), -0.2, 0.2), 0.0, 1.0)
    prim_weight = jnp.clip(jnp.exp(math.log(3.0) - 2.3025851 * jax.random.uniform(arg_keys[1], (NPRIM,), jnp.float32) ** block_levels(arg_keys[1], (NPRIM,), ((0, 256),), -0.2, 0.2)), 0.3, 3.0)
    sec_pos = jnp.clip(1.0 * jax.random.uniform(arg_keys[2], (NBLK, 3, BS), jnp.float32) ** block_levels(arg_keys[2], (NBLK, 3, BS), ((0, 256),), -0.2, 0.2), 0.0, 1.0)
    sec_weight = jnp.clip(jnp.exp(math.log(3.0) - 2.3025851 * jax.random.uniform(arg_keys[3], (NBLK, BS), jnp.float32) ** block_levels(arg_keys[3], (NBLK, BS), ((0, 256),), -0.2, 0.2)), 0.3, 3.0)
    sec_counts = draw_sec_counts(jax.random.fold_in(arg_keys[7], 71), 0)
    tile_lists = draw_tile_lists(jax.random.fold_in(arg_keys[7], 71), 0)
    region_of_keys = jax.random.split(jax.random.fold_in(arg_keys[6], 1), NPRIM // PRIM_DEV)
    region_of_turns = jax.random.permutation(jax.random.fold_in(arg_keys[6], 3), NPRIM // PRIM_DEV)
    region_of = jax.vmap(lambda own, number: deal_out(jax.random.fold_in(arg_keys[6], 2), own, number, PRIM_DEV, REGIONS, 1, CAP, 2))(region_of_keys, region_of_turns).reshape((NPRIM, 1))
    return dict(prim_pos=prim_pos, prim_weight=prim_weight, sec_pos=sec_pos, sec_weight=sec_weight, sec_counts=sec_counts, tile_lists=tile_lists, region_of=region_of)


max_radius = 1.0

def harmonic_table(degree_top):
    table_rows = []
    for m_order in range(degree_top + 1):
        part_kinds = [0] if m_order == 0 else [0, 1]
        for part_kind in part_kinds:
            for degree in range(m_order, degree_top + 1):
                factor = math.sqrt((2 * degree + 1) / (4.0 * math.pi) * math.factorial(degree - m_order) / math.factorial(degree + m_order))
                if m_order > 0:
                    factor = factor * math.sqrt(2.0)
                table_rows.append((m_order, part_kind, degree, factor))
    return table_rows

def order_slices(degree_top, bin_count):
    slices = []
    position = 0
    for m_order in range(degree_top + 1):
        length = (degree_top + 1 - m_order) * bin_count
        if m_order == 0:
            slices.append((position, -1, length))
            position = position + length
        else:
            slices.append((position, position + length, length))
            position = position + 2 * length
    return slices

def angular_basis(separation, degree_top, floor_radius):
    radius = jnp.sqrt(separation[0] * separation[0] + separation[1] * separation[1] + separation[2] * separation[2])
    safe_radius = jnp.maximum(radius, floor_radius)
    unit_x = separation[0] / safe_radius
    unit_y = separation[1] / safe_radius
    cosine = separation[2] / safe_radius
    cos_part = [jnp.ones_like(unit_x)]
    sin_part = [jnp.zeros_like(unit_x)]
    for m_order in range(1, degree_top + 1):
        cos_part.append(cos_part[-1] * unit_x - sin_part[-1] * unit_y)
        sin_part.append(sin_part[-1] * unit_x + cos_part[-2] * unit_y)
    legendre = {}
    for m_order in range(degree_top + 1):
        corner = 1.0
        for odd_value in range(1, 2 * m_order, 2):
            corner = corner * odd_value
        legendre[m_order, m_order] = jnp.full_like(unit_x, corner)
        if m_order < degree_top:
            legendre[m_order + 1, m_order] = (2 * m_order + 1) * cosine * legendre[m_order, m_order]
        for degree in range(m_order + 2, degree_top + 1):
            legendre[degree, m_order] = ((2 * degree - 1) * cosine * legendre[degree - 1, m_order] - (degree + m_order - 1) * legendre[degree - 2, m_order]) / (degree - m_order)
    harmonic_list = []
    for m_order, part_kind, degree, factor in harmonic_table(degree_top):
        angular = cos_part[m_order] if part_kind == 0 else sin_part[m_order]
        harmonic_list.append(factor * legendre[degree, m_order] * angular)
    return (radius, harmonic_list)

def tile_sums(prim_xyz, block_pos, block_weight):
    list_slots, _, width = block_pos.shape
    sec_xyz = jnp.transpose(block_pos, (1, 0, 2)).reshape(3, list_slots * width)
    weight_row = block_weight.reshape(list_slots * width)
    separation = sec_xyz[:, None, :] - prim_xyz[:, :, None]
    bin_step = max_radius / (NBIN + 1)
    radius, harmonic_list = angular_basis(separation, LMAX, 0.5 * bin_step)
    harmonic_rows = jnp.stack(harmonic_list, axis=1).astype(jnp.bfloat16)
    centers = jnp.arange(1, NBIN + 1).astype(jnp.float32)
    spline = jnp.maximum(0.0, 1.0 - jnp.abs(radius[:, None, :] / bin_step - centers[None, :, None]))
    weighted = (spline * weight_row[None, None, :]).astype(jnp.bfloat16)
    harmonic_rows, weighted = lax.optimization_barrier((harmonic_rows, weighted))
    pair_sums = jnp.einsum('pjs,pbs->pjb', harmonic_rows.astype(jnp.float32), weighted.astype(jnp.float32))
    return pair_sums.reshape(pair_sums.shape[0], -1)

def row_products(rows_group):
    pieces = []
    for cos_start, sin_start, length in order_slices(LMAX, NBIN):
        cos_rows = rows_group[:, cos_start:cos_start + length]
        outer_prod = cos_rows[:, :, None] * cos_rows[:, None, :]
        if sin_start >= 0:
            sine_rows = rows_group[:, sin_start:sin_start + length]
            outer_prod = outer_prod + sine_rows[:, :, None] * sine_rows[:, None, :]
        pieces.append(outer_prod.reshape(rows_group.shape[0], -1))
    return jnp.concatenate(pieces, axis=1)

def reference(prim_pos, prim_weight, sec_pos, sec_weight, sec_counts, tile_lists, region_of):
    lane_index = jnp.arange(BS).astype(jnp.int32)
    live_mask = (lane_index[None, :] < sec_counts[:, None]).astype(jnp.float32)
    live_weight = sec_weight * live_mask
    norm_scale = 1.0 / math.sqrt(LIST * BS)
    tile_count = NPRIM // PT
    tile_xyz = prim_pos.reshape(3, tile_count, PT).transpose(1, 0, 2)
    tile_weight = prim_weight.reshape(tile_count, PT)

    def one_tile(tile_args):
        xyz_rows, weight_rows, listed = tile_args
        in_use = listed >= 0
        safe_list = jnp.where(in_use, listed, 0).astype(jnp.int32)
        block_pos = sec_pos[safe_list]
        block_weight = live_weight[safe_list] * in_use.astype(jnp.float32)[:, None]
        pair_sums = tile_sums(xyz_rows, block_pos, block_weight)
        return (pair_sums * (weight_rows * norm_scale)[:, None]).astype(jnp.bfloat16)
    coefficients = lax.map(one_tile, (tile_xyz, tile_weight, tile_lists)).reshape(NPRIM, FEAT)
    regions = region_of[:, 0].astype(jnp.int32)

    def add_group(total, group_args):
        rows_group, region_group = group_args
        products = row_products(rows_group.astype(jnp.float32))
        return (total.at[region_group].add(products), None)
    total, _ = lax.scan(add_group, jnp.zeros((REGIONS, TOTAL), jnp.float32), (coefficients.reshape(-1, PRIM_DEV, FEAT), regions.reshape(-1, PRIM_DEV)))
    return (coefficients, total * (1.0 / PRIM_DEV))
```

```python
import functools
import math

import jax
import jax.numpy as jnp
from jax import lax
from jax.experimental import pallas as pl
from jax.experimental.pallas import tpu as pltpu
from jax.sharding import PartitionSpec as P

LMAX = 10
NBIN = 16
BS = 128
LIST = 12
PT = 16
PRIM_DEV = 64
NHARM = (LMAX + 1) ** 2
FEAT = NHARM * NBIN
WIDE = 2048

GROUPS = ((0, 1), (2, 3), (4, 5, 6), (7, 8, 9, 10))


def padded(cells, sides, width):
    for axis, dim in sides:
        count = lax.axis_size(axis)
        head = lax.slice_in_dim(cells, 0, width, axis=dim)
        tail = lax.slice_in_dim(cells, cells.shape[dim] - width, cells.shape[dim], axis=dim)
        cells = jnp.concatenate(
            [
                lax.ppermute(tail, axis, [(i, (i + 1) % count) for i in range(count)]),
                cells,
                lax.ppermute(head, axis, [((i + 1) % count, i) for i in range(count)]),
            ],
            axis=dim,
        )
    return cells


def order_slices(degree_top, bin_count):
    slices = []
    position = 0
    for m_order in range(degree_top + 1):
        length = (degree_top + 1 - m_order) * bin_count
        if m_order == 0:
            slices.append((position, -1, length))
            position = position + length
        else:
            slices.append((position, position + length, length))
            position = position + 2 * length
    return slices


def harmonic_scale(m_order, degree):
    factor = math.sqrt(
        (2 * degree + 1)
        / (4.0 * math.pi)
        * math.factorial(degree - m_order)
        / math.factorial(degree + m_order)
    )
    if m_order > 0:
        factor = factor * math.sqrt(2.0)
    lead = 1.0
    for odd_value in range(1, 2 * m_order, 2):
        lead = lead * odd_value
    for step in range(m_order + 1, degree + 1):
        lead = lead * (2 * step - 1) / (step - m_order)
    return factor * lead


def first_row(m_order):
    return order_slices(LMAX, 1)[m_order][0]


def pair_kernel(pick_ref, count_ref, pool_ref, prim_ref, coef_ref, packed, basis, spline, acc, diag, spread):
    tile = pl.program_id(0)
    lane = lax.broadcasted_iota(jnp.int32, (8, BS), 1)

    @pl.when(tile == 0)
    def _():
        row = lax.broadcasted_iota(jnp.int32, (PT * NBIN, 128), 0)
        col = lax.broadcasted_iota(jnp.int32, (PT * NBIN, 128), 1)
        for part in range(8):
            spread[part] = jnp.where(col == part * NBIN + row // PT, 1.0, 0.0).astype(jnp.bfloat16)

    packed[...] = jnp.zeros_like(packed)
    filled = jnp.int32(0)
    for slot in range(LIST):
        pick = pick_ref[tile, slot]
        block = pool_ref[jnp.maximum(pick, 0)]
        base = filled // BS
        shift = filled % BS
        moved = pltpu.roll(block, shift, 1)
        used = pick >= 0
        low = jnp.where((lane >= shift) & used, moved, packed[base])
        packed[base] = low
        high = jnp.where((lane < shift) & used, moved, packed[base + 1])
        packed[base + 1] = high
        filled = filled + jnp.where(used, count_ref[jnp.maximum(pick, 0)], 0)
    chunks = (filled + 2 * BS - 1) // (2 * BS)

    acc[...] = jnp.zeros_like(acc)
    prim = prim_ref[...]
    px, py, pz = prim[:, 0:1], prim[:, 1:2], prim[:, 2:3]
    bin_step = 1.0 / (NBIN + 1)

    def chunk_step(chunk, carry):
        geometry = []
        for half in range(2):
            rows = packed[2 * chunk + half]
            dx = rows[0:1, :] - px
            dy = rows[1:2, :] - py
            dz = rows[2:3, :] - pz
            weight = jnp.broadcast_to(rows[3:4, :], (PT, BS))
            radius = jnp.sqrt(dx * dx + dy * dy + dz * dz)
            inverse = 1.0 / jnp.maximum(radius, 0.5 * bin_step)
            geometry.append((dx * inverse, dy * inverse, dz * inverse))
            place = radius * float(NBIN + 1)
            whole = jnp.floor(place)
            part = place - whole
            upper = weight * part
            lower = weight * (1.0 - part)
            cols = slice(half * BS, (half + 1) * BS)
            above = jnp.where(whole == 0.0, upper, 0.0)
            for bin_at in range(NBIN):
                here = whole == float(bin_at + 1)
                spline[bin_at * PT : (bin_at + 1) * PT, cols] = jnp.where(here, lower, above).astype(
                    jnp.bfloat16
                )
                above = jnp.where(here, upper, 0.0)
        angular = [[None, None], [None, None]]
        for orders in GROUPS:
            for half in range(2):
                ux, uy, uz = geometry[half]
                cols = slice(half * BS, (half + 1) * BS)
                for m_order in orders:
                    if m_order == 1:
                        angular[half] = [ux, uy]
                    elif m_order > 1:
                        cos_part, sin_part = angular[half]
                        angular[half] = [
                            cos_part * ux - sin_part * uy,
                            sin_part * ux + cos_part * uy,
                        ]
                    older, newer = None, None
                    start = first_row(m_order)
                    count = LMAX + 1 - m_order
                    for degree in range(m_order, LMAX + 1):
                        if degree == m_order:
                            current = None
                        elif degree == m_order + 1:
                            current = uz
                        else:
                            ratio = (degree + m_order - 1) * (degree - m_order - 1) / (
                                (2 * degree - 1) * (2 * degree - 3)
                            )
                            if older is None:
                                current = uz * newer - ratio
                            else:
                                current = uz * newer - ratio * older
                        older, newer = newer, current
                        scale = harmonic_scale(m_order, degree)
                        at = (start + degree - m_order) * PT
                        if current is None:
                            scaled = None
                        else:
                            scaled = current * scale
                        if m_order == 0:
                            value = jnp.full((PT, BS), scale, jnp.float32) if scaled is None else scaled
                            basis[at : at + PT, cols] = value.astype(jnp.bfloat16)
                        else:
                            for kind in range(2):
                                turn = angular[half][kind]
                                value = turn * scale if scaled is None else scaled * turn
                                low = at + kind * count * PT
                                basis[low : low + PT, cols] = value.astype(jnp.bfloat16)
            first = first_row(orders[0]) * PT
            last = NHARM * PT if orders[-1] == LMAX else first_row(orders[-1] + 1) * PT
            acc[first:last, :] += lax.dot_general(
                basis[first:last, :],
                spline[...],
                (((1,), (1,)), ((), ())),
                preferred_element_type=jnp.float32,
            )
        return carry

    lax.fori_loop(0, chunks, chunk_step, 0)

    row = lax.broadcasted_iota(jnp.int32, (PT, PT * NBIN), 0)
    col = lax.broadcasted_iota(jnp.int32, (PT, PT * NBIN), 1)
    keep = jnp.where(col % PT == row, prim[:, 3:4], 0.0)
    for harm in range(128):
        if harm < NHARM:
            value = (acc[harm * PT : (harm + 1) * PT, :] * keep).astype(jnp.bfloat16)
        else:
            value = jnp.zeros((PT, PT * NBIN), jnp.bfloat16)
        diag[harm % 8, (harm // 8) * PT : (harm // 8 + 1) * PT, :] = value
    total = jnp.zeros((256, 128), jnp.float32)
    for part in range(8):
        total = total + jnp.dot(diag[part], spread[part], preferred_element_type=jnp.float32)
    rows = total.astype(jnp.bfloat16)
    for group in range(15):
        coef_ref[:, group * 128 : (group + 1) * 128] = rows[group * PT : (group + 1) * PT, :]
    coef_ref[:, 1920:FEAT] = rows[15 * PT : 16 * PT, : FEAT - 1920]


def pair_sums(pick, counts, pool, prim):
    tiles = pick.shape[0]
    return pl.pallas_call(
        pair_kernel,
        out_shape=jax.ShapeDtypeStruct((tiles * PT, FEAT), jnp.bfloat16),
        grid_spec=pltpu.PrefetchScalarGridSpec(
            num_scalar_prefetch=2,
            grid=(tiles,),
            in_specs=[
                pl.BlockSpec(pool.shape, lambda t, *_: (0, 0, 0)),
                pl.BlockSpec((PT, prim.shape[1]), lambda t, *_: (t, 0)),
            ],
            out_specs=pl.BlockSpec((PT, FEAT), lambda t, *_: (t, 0)),
            scratch_shapes=[
                pltpu.VMEM((2 * ((LIST + 1) // 2) + 2, 8, BS), jnp.float32),
                pltpu.VMEM((NHARM * PT, 2 * BS), jnp.bfloat16),
                pltpu.VMEM((NBIN * PT, 2 * BS), jnp.bfloat16),
                pltpu.VMEM((NHARM * PT, NBIN * PT), jnp.float32),
                pltpu.VMEM((8, 256, NBIN * PT), jnp.bfloat16),
                pltpu.VMEM((8, NBIN * PT, 128), jnp.bfloat16),
            ],
        ),
        compiler_params=pltpu.CompilerParams(vmem_limit_bytes=40 << 20),
        name="pair_sums",
    )(pick, counts, pool, prim)


def self_product(left_rows, right_rows):
    return lax.dot_general(
        left_rows, right_rows, (((0,), (0,)), ((), ())), preferred_element_type=jnp.float32
    )


def gram_by_order(owner_rows):
    pieces = []
    for cos_start, sin_start, length in order_slices(LMAX, NBIN):
        cos_rows = owner_rows[:, cos_start : cos_start + length]
        gram_block = self_product(cos_rows, cos_rows)
        if sin_start >= 0:
            sine_rows = owner_rows[:, sin_start : sin_start + length]
            gram_block = gram_block + self_product(sine_rows, sine_rows)
        pieces.append(gram_block.reshape(-1))
    return jnp.concatenate(pieces)


def shards(prim_pos, prim_weight, sec_pos, sec_weight, sec_counts, tile_lists, region_of):
    box_count = lax.axis_size("box")
    help_count = lax.axis_size("help")
    per_device = sec_pos.shape[0]
    lane_index = jnp.arange(sec_pos.shape[2], dtype=jnp.int32)
    live_mask = (lane_index[None, :] < sec_counts[:, None]).astype(jnp.float32)
    count_row = jnp.broadcast_to(
        sec_counts.astype(jnp.float32)[:, None, None], (per_device, 4, sec_pos.shape[2])
    )
    own_blocks = jnp.concatenate(
        [sec_pos, (sec_weight * live_mask)[:, None, :], count_row], axis=1
    )
    chip_pool = lax.all_gather(own_blocks, "help", axis=0, tiled=True)
    block_pool = padded(chip_pool, (("box", 0),), chip_pool.shape[0])
    pool_counts = block_pool[:, 4, 0].astype(jnp.int32)
    in_use = tile_lists >= 0
    safe_list = jnp.where(in_use, tile_lists, 0)
    owner_dev = safe_list // per_device
    box_move = jnp.mod(owner_dev // help_count - lax.axis_index("box") + 1, box_count)
    pool_index = (
        box_move * (help_count * per_device)
        + owner_dev % help_count * per_device
        + safe_list % per_device
    )
    pool_index = jnp.where(in_use, pool_index, -1).astype(jnp.int32)
    row_total = prim_pos.shape[1]
    norm_scale = 1.0 / math.sqrt(LIST * BS)
    prim = jnp.concatenate([prim_pos, (prim_weight * norm_scale)[None, :]], axis=0).T

    coefficients = pair_sums(pool_index, pool_counts, block_pool, prim)
    feat_width = coefficients.shape[1]
    capacity = max(2, 2 * row_total // (box_count * help_count))
    regions = region_of[:, 0]
    row_order = jnp.arange(row_total, dtype=jnp.int32)
    earlier = row_order[:, None] > row_order[None, :]
    same_region = regions[:, None] == regions[None, :]
    row_rank = jnp.sum((earlier & same_region).astype(jnp.int32), axis=1)
    row_slots = regions * capacity + row_rank
    outgoing = (
        jnp.zeros((box_count * help_count * capacity, feat_width), jnp.bfloat16)
        .at[row_slots]
        .set(coefficients)
    )
    outgoing = outgoing.reshape(box_count, help_count, capacity, feat_width)
    incoming = lax.all_to_all(
        lax.all_to_all(outgoing, "box", split_axis=0, concat_axis=0, tiled=True),
        "help",
        split_axis=1,
        concat_axis=1,
        tiled=True,
    )
    owner_rows = incoming.reshape(-1, feat_width)
    region_sum = gram_by_order(owner_rows)
    region_tensor = (region_sum * (1.0 / PRIM_DEV)).reshape(1, -1)
    return (coefficients, region_tensor)


def solution(mesh):
    placed = (
        P(None, ("box", "help")),
        P(("box", "help")),
        P(("box", "help"), None, None),
        P(("box", "help"), None),
        P(("box", "help")),
        P(("box", "help"), None),
        P(("box", "help"), None),
    )
    return jax.shard_map(
        shards,
        mesh=mesh,
        in_specs=placed,
        out_specs=(P(("box", "help"), None), P(("box", "help"), None)),
        check_vma=False,
    )
```

```python
import functools
import math

import jax
import jax.numpy as jnp
from jax import lax
from jax.experimental import pallas as pl
from jax.experimental.pallas import tpu as pltpu
from jax.sharding import PartitionSpec as P

LMAX = 10
NBIN = 16
BS = 128
LIST = 12
PT = 16
PRIM_DEV = 64
NHARM = (LMAX + 1) ** 2
FEAT = NHARM * NBIN
WIDE = 2048

GROUPS = ((0, 1), (2, 3), (4, 5, 6), (7, 8, 9, 10))


def padded(cells, sides, width):
    for axis, dim in sides:
        count = lax.axis_size(axis)
        head = lax.slice_in_dim(cells, 0, width, axis=dim)
        tail = lax.slice_in_dim(cells, cells.shape[dim] - width, cells.shape[dim], axis=dim)
        cells = jnp.concatenate(
            [
                lax.ppermute(tail, axis, [(i, (i + 1) % count) for i in range(count)]),
                cells,
                lax.ppermute(head, axis, [((i + 1) % count, i) for i in range(count)]),
            ],
            axis=dim,
        )
    return cells


def order_slices(degree_top, bin_count):
    slices = []
    position = 0
    for m_order in range(degree_top + 1):
        length = (degree_top + 1 - m_order) * bin_count
        if m_order == 0:
            slices.append((position, -1, length))
            position = position + length
        else:
            slices.append((position, position + length, length))
            position = position + 2 * length
    return slices


def harmonic_scale(m_order, degree):
    factor = math.sqrt(
        (2 * degree + 1)
        / (4.0 * math.pi)
        * math.factorial(degree - m_order)
        / math.factorial(degree + m_order)
    )
    if m_order > 0:
        factor = factor * math.sqrt(2.0)
    lead = 1.0
    for odd_value in range(1, 2 * m_order, 2):
        lead = lead * odd_value
    for step in range(m_order + 1, degree + 1):
        lead = lead * (2 * step - 1) / (step - m_order)
    return factor * lead


def first_row(m_order):
    return order_slices(LMAX, 1)[m_order][0]


def pair_kernel(pick_ref, count_ref, pool_ref, prim_ref, coef_ref, packed, basis, spline, acc, diag, spread):
    tile = pl.program_id(0)
    lane = lax.broadcasted_iota(jnp.int32, (8, BS), 1)

    @pl.when(tile == 0)
    def _():
        row = lax.broadcasted_iota(jnp.int32, (PT * NBIN, 128), 0)
        col = lax.broadcasted_iota(jnp.int32, (PT * NBIN, 128), 1)
        for part in range(8):
            spread[part] = jnp.where(col == part * NBIN + row // PT, 1.0, 0.0).astype(jnp.bfloat16)

    packed[...] = jnp.zeros_like(packed)
    filled = jnp.int32(0)
    for slot in range(LIST):
        pick = pick_ref[tile, slot]
        block = pool_ref[jnp.maximum(pick, 0)]
        base = filled // BS
        shift = filled % BS
        moved = pltpu.roll(block, shift, 1)
        used = pick >= 0
        low = jnp.where((lane >= shift) & used, moved, packed[base])
        packed[base] = low
        high = jnp.where((lane < shift) & used, moved, packed[base + 1])
        packed[base + 1] = high
        filled = filled + jnp.where(used, count_ref[jnp.maximum(pick, 0)], 0)
    chunks = (filled + 2 * BS - 1) // (2 * BS)

    acc[...] = jnp.zeros_like(acc)
    prim = prim_ref[...]
    px, py, pz = prim[:, 0:1], prim[:, 1:2], prim[:, 2:3]
    bin_step = 1.0 / (NBIN + 1)

    def chunk_step(chunk, carry):
        geometry = []
        for half in range(2):
            rows = packed[2 * chunk + half]
            dx = rows[0:1, :] - px
            dy = rows[1:2, :] - py
            dz = rows[2:3, :] - pz
            weight = jnp.broadcast_to(rows[3:4, :], (PT, BS))
            radius = jnp.sqrt(dx * dx + dy * dy + dz * dz)
            inverse = 1.0 / jnp.maximum(radius, 0.5 * bin_step)
            geometry.append((dx * inverse, dy * inverse, dz * inverse))
            place = radius * float(NBIN + 1)
            whole = jnp.floor(place)
            part = place - whole
            upper = weight * part
            lower = weight * (1.0 - part)
            cols = slice(half * BS, (half + 1) * BS)
            above = jnp.where(whole == 0.0, upper, 0.0)
            for bin_at in range(NBIN):
                here = whole == float(bin_at + 1)
                spline[bin_at * PT : (bin_at + 1) * PT, cols] = jnp.where(here, lower, above).astype(
                    jnp.bfloat16
                )
                above = jnp.where(here, upper, 0.0)
        angular = [[None, None], [None, None]]
        for orders in GROUPS:
            for half in range(2):
                ux, uy, uz = geometry[half]
                cols = slice(half * BS, (half + 1) * BS)
                for m_order in orders:
                    if m_order == 1:
                        angular[half] = [ux, uy]
                    elif m_order > 1:
                        cos_part, sin_part = angular[half]
                        angular[half] = [
                            cos_part * ux - sin_part * uy,
                            sin_part * ux + cos_part * uy,
                        ]
                    older, newer = None, None
                    start = first_row(m_order)
                    count = LMAX + 1 - m_order
                    for degree in range(m_order, LMAX + 1):
                        if degree == m_order:
                            current = None
                        elif degree == m_order + 1:
                            current = uz
                        else:
                            ratio = (degree + m_order - 1) * (degree - m_order - 1) / (
                                (2 * degree - 1) * (2 * degree - 3)
                            )
                            if older is None:
                                current = uz * newer - ratio
                            else:
                                current = uz * newer - ratio * older
                        older, newer = newer, current
                        scale = harmonic_scale(m_order, degree)
                        at = (start + degree - m_order) * PT
                        if current is None:
                            scaled = None
                        else:
                            scaled = current * scale
                        if m_order == 0:
                            value = jnp.full((PT, BS), scale, jnp.float32) if scaled is None else scaled
                            basis[at : at + PT, cols] = value.astype(jnp.bfloat16)
                        else:
                            for kind in range(2):
                                turn = angular[half][kind]
                                value = turn * scale if scaled is None else scaled * turn
                                low = at + kind * count * PT
                                basis[low : low + PT, cols] = value.astype(jnp.bfloat16)
            first = first_row(orders[0]) * PT
            last = NHARM * PT if orders[-1] == LMAX else first_row(orders[-1] + 1) * PT
            acc[first:last, :] += lax.dot_general(
                basis[first:last, :],
                spline[...],
                (((1,), (1,)), ((), ())),
                preferred_element_type=jnp.float32,
            )
        return carry

    lax.fori_loop(0, chunks, chunk_step, 0)

    row = lax.broadcasted_iota(jnp.int32, (PT, PT * NBIN), 0)
    col = lax.broadcasted_iota(jnp.int32, (PT, PT * NBIN), 1)
    keep = jnp.where(col % PT == row, prim[:, 3:4], 0.0)
    for harm in range(128):
        if harm < NHARM:
            value = (acc[harm * PT : (harm + 1) * PT, :] * keep).astype(jnp.bfloat16)
        else:
            value = jnp.zeros((PT, PT * NBIN), jnp.bfloat16)
        diag[harm % 8, (harm // 8) * PT : (harm // 8 + 1) * PT, :] = value
    total = jnp.zeros((256, 128), jnp.float32)
    for part in range(8):
        total = total + jnp.dot(diag[part], spread[part], preferred_element_type=jnp.float32)
    rows = total.astype(jnp.bfloat16)
    for group in range(15):
        coef_ref[:, group * 128 : (group + 1) * 128] = rows[group * PT : (group + 1) * PT, :]
    coef_ref[:, 1920:FEAT] = rows[15 * PT : 16 * PT, : FEAT - 1920]


def pair_sums(pick, counts, pool, prim):
    tiles = pick.shape[0]
    return pl.pallas_call(
        pair_kernel,
        out_shape=jax.ShapeDtypeStruct((tiles * PT, FEAT), jnp.bfloat16),
        grid_spec=pltpu.PrefetchScalarGridSpec(
            num_scalar_prefetch=2,
            grid=(tiles,),
            in_specs=[
                pl.BlockSpec(pool.shape, lambda t, *_: (0, 0, 0)),
                pl.BlockSpec((PT, prim.shape[1]), lambda t, *_: (t, 0)),
            ],
            out_specs=pl.BlockSpec((PT, FEAT), lambda t, *_: (t, 0)),
            scratch_shapes=[
                pltpu.VMEM((2 * ((LIST + 1) // 2) + 2, 8, BS), jnp.float32),
                pltpu.VMEM((NHARM * PT, 2 * BS), jnp.bfloat16),
                pltpu.VMEM((NBIN * PT, 2 * BS), jnp.bfloat16),
                pltpu.VMEM((NHARM * PT, NBIN * PT), jnp.float32),
                pltpu.VMEM((8, 256, NBIN * PT), jnp.bfloat16),
                pltpu.VMEM((8, NBIN * PT, 128), jnp.bfloat16),
            ],
        ),
        compiler_params=pltpu.CompilerParams(vmem_limit_bytes=40 << 20),
        name="pair_sums",
    )(pick, counts, pool, prim)


def gram_kernel(rows_ref, out_ref, feats, gram):
    row_total = rows_ref.shape[0]
    row = lax.broadcasted_iota(jnp.int32, (256, 256), 0)
    col = lax.broadcasted_iota(jnp.int32, (256, 256), 1)
    turn = jnp.where(col == (row % 16) * 16 + row // 16, 1.0, 0.0).astype(jnp.bfloat16)

    def regroup(step, carry):
        at = pl.multiple_of(step * 16, 16)
        block = rows_ref[pl.ds(at, 16)].reshape(256, 128)
        moved = jnp.dot(turn, block, preferred_element_type=jnp.float32).astype(jnp.bfloat16)
        feats[:, pl.ds(at, 16), :] = moved.reshape(16, 16, 128)
        return carry

    lax.fori_loop(0, row_total // 16, regroup, 0)
    row = lax.broadcasted_iota(jnp.int32, (128, 128), 0)
    col = lax.broadcasted_iota(jnp.int32, (128, 128), 1)

    def one_hot(cond):
        return jnp.where(cond, 1.0, 0.0).astype(jnp.bfloat16)

    def aligned(start, width):
        group, skip = start // 128, start % 128
        here, there = one_hot(row == col + skip), one_hot(row + 128 == col + skip)
        here_t, there_t = one_hot(col == row + skip), one_hot(col + 128 == row + skip)
        across = (((1,), (1,)), ((), ()))
        plain = jnp.dot(feats[group], here, preferred_element_type=jnp.float32)
        flipped = lax.dot_general(here_t, feats[group], across, preferred_element_type=jnp.float32)
        if skip + width > 128:
            plain += jnp.dot(feats[group + 1], there, preferred_element_type=jnp.float32)
            flipped += lax.dot_general(
                there_t, feats[group + 1], across, preferred_element_type=jnp.float32
            )
        return plain.astype(jnp.bfloat16), flipped.astype(jnp.bfloat16)

    base = 0
    for cos_start, sin_start, length in order_slices(LMAX, NBIN):
        count = length // NBIN
        parts = -(-length // 128)
        for kind_start in (cos_start, sin_start):
            if kind_start < 0:
                continue
            tiles = [
                aligned(kind_start + 128 * part, min(128, length - 128 * part))
                for part in range(parts)
            ]
            for up in range(parts):
                for over in range(parts):
                    product = jnp.dot(
                        tiles[up][1], tiles[over][0], preferred_element_type=jnp.float32
                    )
                    at = (over, slice(up * 128, up * 128 + 128))
                    if kind_start == cos_start:
                        gram[at] = product
                    else:
                        gram[at] += product
        lane = lax.broadcasted_iota(jnp.int32, (2 * count, 128), 1)
        for rest in range(8):
            for part in range(parts):
                units = min(8, count - 8 * part)
                shift = rest * count % 8
                at = base + rest * count // 8 + part
                value = gram[part, pl.ds(rest, 2 * count, stride=8), :] * (1.0 / PRIM_DEV)
                if shift:
                    value = pltpu.roll(value, 16 * shift, 1)
                window = pl.ds(at, 2 * count, stride=count)
                keep = (lane >= 16 * shift) & (lane < 16 * (shift + units))
                out_ref[window, :] = jnp.where(keep, value, out_ref[window, :])
                if shift + units > 8:
                    window = pl.ds(at + 1, 2 * count, stride=count)
                    keep = lane < 16 * (shift + units - 8)
                    out_ref[window, :] = jnp.where(keep, value, out_ref[window, :])
        base += 2 * count * count


def gram_rows(rows):
    total = sum(length * length for _, _, length in order_slices(LMAX, NBIN))
    return pl.pallas_call(
        gram_kernel,
        out_shape=jax.ShapeDtypeStruct((total // 128, 128), jnp.float32),
        in_specs=[pl.BlockSpec(memory_space=pltpu.VMEM)],
        out_specs=pl.BlockSpec(memory_space=pltpu.VMEM),
        scratch_shapes=[
            pltpu.VMEM((16, rows.shape[0], 128), jnp.bfloat16),
            pltpu.VMEM((2, 256, 128), jnp.float32),
        ],
        compiler_params=pltpu.CompilerParams(vmem_limit_bytes=40 << 20),
        name="gram_rows",
    )(rows)


def shards(prim_pos, prim_weight, sec_pos, sec_weight, sec_counts, tile_lists, region_of):
    box_count = lax.axis_size("box")
    help_count = lax.axis_size("help")
    per_device = sec_pos.shape[0]
    lane_index = jnp.arange(sec_pos.shape[2], dtype=jnp.int32)
    live_mask = (lane_index[None, :] < sec_counts[:, None]).astype(jnp.float32)
    count_row = jnp.broadcast_to(
        sec_counts.astype(jnp.float32)[:, None, None], (per_device, 4, sec_pos.shape[2])
    )
    own_blocks = jnp.concatenate(
        [sec_pos, (sec_weight * live_mask)[:, None, :], count_row], axis=1
    )
    chip_pool = lax.all_gather(own_blocks, "help", axis=0, tiled=True)
    block_pool = padded(chip_pool, (("box", 0),), chip_pool.shape[0])
    pool_counts = block_pool[:, 4, 0].astype(jnp.int32)
    in_use = tile_lists >= 0
    safe_list = jnp.where(in_use, tile_lists, 0)
    owner_dev = safe_list // per_device
    box_move = jnp.mod(owner_dev // help_count - lax.axis_index("box") + 1, box_count)
    pool_index = (
        box_move * (help_count * per_device)
        + owner_dev % help_count * per_device
        + safe_list % per_device
    )
    pool_index = jnp.where(in_use, pool_index, -1).astype(jnp.int32)
    row_total = prim_pos.shape[1]
    norm_scale = 1.0 / math.sqrt(LIST * BS)
    prim = jnp.concatenate([prim_pos, (prim_weight * norm_scale)[None, :]], axis=0).T

    coefficients = pair_sums(pool_index, pool_counts, block_pool, prim)
    feat_width = coefficients.shape[1]
    capacity = max(2, 2 * row_total // (box_count * help_count))
    regions = region_of[:, 0]
    row_order = jnp.arange(row_total, dtype=jnp.int32)
    earlier = row_order[:, None] > row_order[None, :]
    same_region = regions[:, None] == regions[None, :]
    row_rank = jnp.sum((earlier & same_region).astype(jnp.int32), axis=1)
    row_slots = regions * capacity + row_rank
    outgoing = (
        jnp.zeros((box_count * help_count * capacity, feat_width), jnp.bfloat16)
        .at[row_slots]
        .set(coefficients)
    )
    outgoing = outgoing.reshape(box_count, help_count, capacity, feat_width)
    incoming = lax.all_to_all(
        lax.all_to_all(outgoing, "box", split_axis=0, concat_axis=0, tiled=True),
        "help",
        split_axis=1,
        concat_axis=1,
        tiled=True,
    )
    owner_rows = incoming.reshape(-1, feat_width)
    owner_rows = jnp.pad(owner_rows, ((0, 0), (0, WIDE - feat_width))).reshape(-1, 16, 128)
    region_tensor = gram_rows(owner_rows).reshape(1, -1)
    return (coefficients, region_tensor)


def solution(mesh):
    placed = (
        P(None, ("box", "help")),
        P(("box", "help")),
        P(("box", "help"), None, None),
        P(("box", "help"), None),
        P(("box", "help")),
        P(("box", "help"), None),
        P(("box", "help"), None),
    )
    return jax.shard_map(
        shards,
        mesh=mesh,
        in_specs=placed,
        out_specs=(P(("box", "help"), None), P(("box", "help"), None)),
        check_vma=False,
    )
```

```python
import functools
import math

import jax
import jax.numpy as jnp
from jax import lax
from jax.experimental import pallas as pl
from jax.experimental.pallas import tpu as pltpu
from jax.sharding import PartitionSpec as P

LMAX = 10
NBIN = 16
BS = 128
LIST = 12
PT = 16
PRIM_DEV = 64
NHARM = (LMAX + 1) ** 2
FEAT = NHARM * NBIN
WIDE = 2048

GROUPS = ((0, 1), (2, 3), (4, 5, 6), (7, 8, 9, 10))


def padded(cells, sides, width):
    for axis, dim in sides:
        count = lax.axis_size(axis)
        head = lax.slice_in_dim(cells, 0, width, axis=dim)
        tail = lax.slice_in_dim(cells, cells.shape[dim] - width, cells.shape[dim], axis=dim)
        cells = jnp.concatenate(
            [
                lax.ppermute(tail, axis, [(i, (i + 1) % count) for i in range(count)]),
                cells,
                lax.ppermute(head, axis, [((i + 1) % count, i) for i in range(count)]),
            ],
            axis=dim,
        )
    return cells


def order_slices(degree_top, bin_count):
    slices = []
    position = 0
    for m_order in range(degree_top + 1):
        length = (degree_top + 1 - m_order) * bin_count
        if m_order == 0:
            slices.append((position, -1, length))
            position = position + length
        else:
            slices.append((position, position + length, length))
            position = position + 2 * length
    return slices


def harmonic_scale(m_order, degree):
    factor = math.sqrt(
        (2 * degree + 1)
        / (4.0 * math.pi)
        * math.factorial(degree - m_order)
        / math.factorial(degree + m_order)
    )
    if m_order > 0:
        factor = factor * math.sqrt(2.0)
    lead = 1.0
    for odd_value in range(1, 2 * m_order, 2):
        lead = lead * odd_value
    for step in range(m_order + 1, degree + 1):
        lead = lead * (2 * step - 1) / (step - m_order)
    return factor * lead


def first_row(m_order):
    return order_slices(LMAX, 1)[m_order][0]


def turn_matrix():
    row = lax.broadcasted_iota(jnp.int32, (256, 256), 0)
    col = lax.broadcasted_iota(jnp.int32, (256, 256), 1)
    return jnp.where(col == (row % 16) * 16 + row // 16, 1.0, 0.0).astype(jnp.bfloat16)


def pair_kernel(
    pick_ref, count_ref, pool_ref, prim_ref, coef_ref, rows_ref, packed, basis, spline, acc, diag, spread
):
    tile = pl.program_id(0)
    lane = lax.broadcasted_iota(jnp.int32, (8, BS), 1)

    @pl.when(tile == 0)
    def _():
        row = lax.broadcasted_iota(jnp.int32, (PT * NBIN, 128), 0)
        col = lax.broadcasted_iota(jnp.int32, (PT * NBIN, 128), 1)
        for part in range(8):
            spread[part] = jnp.where(col == part * NBIN + row // PT, 1.0, 0.0).astype(jnp.bfloat16)

    packed[...] = jnp.zeros_like(packed)
    filled = jnp.int32(0)
    for slot in range(LIST):
        pick = pick_ref[tile, slot]
        block = pool_ref[jnp.maximum(pick, 0)]
        base = filled // BS
        shift = filled % BS
        moved = pltpu.roll(block, shift, 1)
        used = pick >= 0
        low = jnp.where((lane >= shift) & used, moved, packed[base])
        packed[base] = low
        high = jnp.where((lane < shift) & used, moved, packed[base + 1])
        packed[base + 1] = high
        filled = filled + jnp.where(used, count_ref[jnp.maximum(pick, 0)], 0)
    chunks = (filled + 2 * BS - 1) // (2 * BS)

    acc[...] = jnp.zeros_like(acc)
    prim = prim_ref[...]
    px, py, pz = prim[:, 0:1], prim[:, 1:2], prim[:, 2:3]
    bin_step = 1.0 / (NBIN + 1)

    def chunk_step(chunk, carry):
        geometry = []
        for half in range(2):
            rows = packed[2 * chunk + half]
            dx = rows[0:1, :] - px
            dy = rows[1:2, :] - py
            dz = rows[2:3, :] - pz
            weight = jnp.broadcast_to(rows[3:4, :], (PT, BS))
            radius = jnp.sqrt(dx * dx + dy * dy + dz * dz)
            inverse = 1.0 / jnp.maximum(radius, 0.5 * bin_step)
            geometry.append((dx * inverse, dy * inverse, dz * inverse))
            place = radius * float(NBIN + 1)
            whole = jnp.floor(place)
            part = place - whole
            upper = weight * part
            lower = weight * (1.0 - part)
            cols = slice(half * BS, (half + 1) * BS)
            above = jnp.where(whole == 0.0, upper, 0.0)
            for bin_at in range(NBIN):
                here = whole == float(bin_at + 1)
                spline[bin_at * PT : (bin_at + 1) * PT, cols] = jnp.where(here, lower, above).astype(
                    jnp.bfloat16
                )
                above = jnp.where(here, upper, 0.0)
        angular = [[None, None], [None, None]]
        for orders in GROUPS:
            for half in range(2):
                ux, uy, uz = geometry[half]
                cols = slice(half * BS, (half + 1) * BS)
                for m_order in orders:
                    if m_order == 1:
                        angular[half] = [ux, uy]
                    elif m_order > 1:
                        cos_part, sin_part = angular[half]
                        angular[half] = [
                            cos_part * ux - sin_part * uy,
                            sin_part * ux + cos_part * uy,
                        ]
                    older, newer = None, None
                    start = first_row(m_order)
                    count = LMAX + 1 - m_order
                    for degree in range(m_order, LMAX + 1):
                        if degree == m_order:
                            current = None
                        elif degree == m_order + 1:
                            current = uz
                        else:
                            ratio = (degree + m_order - 1) * (degree - m_order - 1) / (
                                (2 * degree - 1) * (2 * degree - 3)
                            )
                            if older is None:
                                current = uz * newer - ratio
                            else:
                                current = uz * newer - ratio * older
                        older, newer = newer, current
                        scale = harmonic_scale(m_order, degree)
                        at = (start + degree - m_order) * PT
                        if current is None:
                            scaled = None
                        else:
                            scaled = current * scale
                        if m_order == 0:
                            value = jnp.full((PT, BS), scale, jnp.float32) if scaled is None else scaled
                            basis[at : at + PT, cols] = value.astype(jnp.bfloat16)
                        else:
                            for kind in range(2):
                                turn = angular[half][kind]
                                value = turn * scale if scaled is None else scaled * turn
                                low = at + kind * count * PT
                                basis[low : low + PT, cols] = value.astype(jnp.bfloat16)
            first = first_row(orders[0]) * PT
            last = NHARM * PT if orders[-1] == LMAX else first_row(orders[-1] + 1) * PT
            acc[first:last, :] += lax.dot_general(
                basis[first:last, :],
                spline[...],
                (((1,), (1,)), ((), ())),
                preferred_element_type=jnp.float32,
            )
        return carry

    lax.fori_loop(0, chunks, chunk_step, 0)

    row = lax.broadcasted_iota(jnp.int32, (PT, PT * NBIN), 0)
    col = lax.broadcasted_iota(jnp.int32, (PT, PT * NBIN), 1)
    keep = jnp.where(col % PT == row, prim[:, 3:4], 0.0)
    for harm in range(128):
        if harm < NHARM:
            value = (acc[harm * PT : (harm + 1) * PT, :] * keep).astype(jnp.bfloat16)
        else:
            value = jnp.zeros((PT, PT * NBIN), jnp.bfloat16)
        diag[harm % 8, (harm // 8) * PT : (harm // 8 + 1) * PT, :] = value
    total = jnp.zeros((256, 128), jnp.float32)
    for part in range(8):
        total = total + jnp.dot(diag[part], spread[part], preferred_element_type=jnp.float32)
    rows = total.astype(jnp.bfloat16)
    for group in range(15):
        coef_ref[:, group * 128 : (group + 1) * 128] = rows[group * PT : (group + 1) * PT, :]
    coef_ref[:, 1920:FEAT] = rows[15 * PT : 16 * PT, : FEAT - 1920]
    turned = jnp.dot(turn_matrix(), rows, preferred_element_type=jnp.float32)
    rows_ref[...] = turned.astype(jnp.bfloat16).reshape(PT, 16, 128)


def pair_sums(pick, counts, pool, prim):
    tiles = pick.shape[0]
    return pl.pallas_call(
        pair_kernel,
        out_shape=(
            jax.ShapeDtypeStruct((tiles * PT, FEAT), jnp.bfloat16),
            jax.ShapeDtypeStruct((tiles * PT, 16, 128), jnp.bfloat16),
        ),
        grid_spec=pltpu.PrefetchScalarGridSpec(
            num_scalar_prefetch=2,
            grid=(tiles,),
            in_specs=[
                pl.BlockSpec(pool.shape, lambda t, *_: (0, 0, 0)),
                pl.BlockSpec((PT, prim.shape[1]), lambda t, *_: (t, 0)),
            ],
            out_specs=(
                pl.BlockSpec((PT, FEAT), lambda t, *_: (t, 0)),
                pl.BlockSpec((PT, 16, 128), lambda t, *_: (t, 0, 0)),
            ),
            scratch_shapes=[
                pltpu.VMEM((2 * ((LIST + 1) // 2) + 2, 8, BS), jnp.float32),
                pltpu.VMEM((NHARM * PT, 2 * BS), jnp.bfloat16),
                pltpu.VMEM((NBIN * PT, 2 * BS), jnp.bfloat16),
                pltpu.VMEM((NHARM * PT, NBIN * PT), jnp.float32),
                pltpu.VMEM((8, 256, NBIN * PT), jnp.bfloat16),
                pltpu.VMEM((8, NBIN * PT, 128), jnp.bfloat16),
            ],
        ),
        compiler_params=pltpu.CompilerParams(vmem_limit_bytes=40 << 20),
        name="pair_sums",
    )(pick, counts, pool, prim)


Z_SIZE = 8
PLANE = 16
SOURCE_MOVES = (0, -1, 1, -2, 2, -3, 3, 4)
PEERS = 2 * PLANE
MESH = pl.DeviceIdType.MESH


def exchange_kernel(table_ref, rows_ref, out_ref, *scratch):
    held = (rows_ref,) + scratch[:7]
    stage, ring_send, ring_recv, plane_send, plane_recv = scratch[7:]
    box, core = lax.axis_index("box"), lax.axis_index("help")
    z_at, x_at, y_at = box // PLANE, (box // 4) % 4, box % 4
    ring = (
        ((z_at + 1) % Z_SIZE * PLANE + box % PLANE, core),
        ((z_at + Z_SIZE - 1) % Z_SIZE * PLANE + box % PLANE, core),
    )

    def peer(turn):
        x_to, y_to = (x_at + turn // 8) % 4, (y_at + turn // 2 % 4) % 4
        return (z_at * PLANE + x_to * 4 + y_to, (core + turn % 2) % 2)

    barrier = pltpu.get_barrier_semaphore()
    for way in range(2):
        pl.semaphore_signal(barrier, inc=1, device_id=ring[way], device_id_type=MESH)

    def greet(turn, carry):
        pl.semaphore_signal(barrier, inc=1, device_id=peer(turn), device_id_type=MESH)
        return carry

    lax.fori_loop(1, PEERS, greet, 0)
    pl.semaphore_wait(barrier, PEERS + 1)

    def ring_copy(way, step, half):
        from_at = 0 if step == 1 else 2 * (step - 1) - 1 + way
        to_at = 7 if step == 4 else 2 * step - 1 + way
        part = pl.ds(half * (PRIM_DEV // 2), PRIM_DEV // 2)
        return pltpu.make_async_remote_copy(
            src_ref=held[from_at].at[part],
            dst_ref=held[to_at].at[part],
            send_sem=ring_send.at[way, step - 1, half],
            recv_sem=ring_recv.at[way, step - 1, half],
            device_id=ring[way],
            device_id_type=MESH,
        )

    def deal(batch, first, number):
        def fill(turn, target):
            for source in range(first, first + number):
                z_from = (z_at + SOURCE_MOVES[source] + Z_SIZE) % Z_SIZE
                for slot in range(2):
                    row = table_ref[z_from * (2 * PEERS) + turn * 2 + slot]
                    value = held[source][jnp.maximum(row, 0)]
                    target[turn, source, slot] = jnp.where(row >= 0, value, jnp.zeros_like(value))

        fill(0, out_ref)

        def one_peer(count, carry):
            turn = count * 13 % PEERS
            fill(turn, stage)
            pltpu.make_async_remote_copy(
                src_ref=stage.at[turn, pl.ds(first, number)],
                dst_ref=out_ref.at[turn, pl.ds(first, number)],
                send_sem=plane_send.at[batch],
                recv_sem=plane_recv.at[batch],
                device_id=peer(turn),
                device_id_type=MESH,
            ).start()
            return carry

        lax.fori_loop(1, PEERS, one_peer, 0)

    for half in range(2):
        for way in range(2):
            ring_copy(way, 1, half).start()
    deal(0, 0, 1)
    for step in range(1, 4):
        for half in range(2):
            for way in range(2):
                ring_copy(way, step, half).wait_recv()
                if step < 3 or half == way:
                    ring_copy(way, step + 1, half).start()
        deal(step, 2 * step - 1, 2)
    for way in range(2):
        ring_copy(way, 4, way).wait_recv()
    deal(4, 7, 1)
    for step in range(1, 5):
        for half in range(2):
            for way in range(2):
                if step < 4 or half == way:
                    ring_copy(way, step, half).wait_send()
    for batch, first, number in ((0, 0, 1), (1, 1, 2), (2, 3, 2), (3, 5, 2), (4, 7, 1)):
        sent = stage.at[pl.ds(1, PEERS - 1), pl.ds(first, number)]
        pltpu.make_async_copy(sent, sent, plane_send.at[batch]).wait()
        come = out_ref.at[pl.ds(1, PEERS - 1), pl.ds(first, number)]
        pltpu.make_async_copy(come, come, plane_recv.at[batch]).wait()


def exchange(table, rows):
    shape = (PEERS, Z_SIZE, 2, 16, 128)
    return pl.pallas_call(
        exchange_kernel,
        out_shape=jax.ShapeDtypeStruct(shape, rows.dtype),
        in_specs=[
            pl.BlockSpec(memory_space=pltpu.SMEM),
            pl.BlockSpec(memory_space=pltpu.VMEM),
        ],
        out_specs=pl.BlockSpec(memory_space=pltpu.VMEM),
        scratch_shapes=[pltpu.VMEM(rows.shape, rows.dtype)] * 7
        + [
            pltpu.VMEM(shape, rows.dtype),
            pltpu.SemaphoreType.DMA((2, 4, 2)),
            pltpu.SemaphoreType.DMA((2, 4, 2)),
            pltpu.SemaphoreType.DMA((5,)),
            pltpu.SemaphoreType.DMA((5,)),
        ],
        compiler_params=pltpu.CompilerParams(
            collective_id=1, has_side_effects=True, vmem_limit_bytes=40 << 20
        ),
        name="exchange",
    )(table, rows)


def row_table(regions):
    box, core = lax.axis_index("box"), lax.axis_index("help")
    row_total = regions.shape[0]
    row_order = jnp.arange(row_total, dtype=jnp.int32)
    earlier = row_order[:, None] > row_order[None, :]
    same_region = regions[:, None] == regions[None, :]
    row_rank = jnp.sum((earlier & same_region).astype(jnp.int32), axis=1)
    code = regions * 2 + row_rank
    lines = [[at + PLANE * z for z in range(Z_SIZE)] for at in range(PLANE)]
    codes = lax.all_gather(code, "box", axis_index_groups=lines)
    turn = jnp.arange(PEERS, dtype=jnp.int32)
    x_to, y_to = (box // 4 + turn // 8) % 4, (box + turn // 2) % 4
    owner = (box // PLANE * PLANE + x_to * 4 + y_to) * 2 + (core + turn) % 2
    wanted = (owner[:, None] * 2 + jnp.arange(2, dtype=jnp.int32)[None, :]).reshape(-1)
    found = codes[:, None, :] == wanted[None, :, None]
    return jnp.max(jnp.where(found, row_order[None, None, :], -1), axis=2).reshape(-1)


def gram_kernel(rows_ref, out_ref, feats, gram):
    row_total = rows_ref.shape[0]
    turn = turn_matrix()

    def regroup(step, carry):
        at = pl.multiple_of(step * 16, 16)
        block = rows_ref[pl.ds(at, 16)].reshape(256, 128)
        moved = jnp.dot(turn, block, preferred_element_type=jnp.float32).astype(jnp.bfloat16)
        feats[:, pl.ds(at, 16), :] = moved.reshape(16, 16, 128)
        return carry

    lax.fori_loop(0, row_total // 16, regroup, 0)
    row = lax.broadcasted_iota(jnp.int32, (128, 128), 0)
    col = lax.broadcasted_iota(jnp.int32, (128, 128), 1)

    def one_hot(cond):
        return jnp.where(cond, 1.0, 0.0).astype(jnp.bfloat16)

    def aligned(start, width):
        group, skip = start // 128, start % 128
        here, there = one_hot(row == col + skip), one_hot(row + 128 == col + skip)
        here_t, there_t = one_hot(col == row + skip), one_hot(col + 128 == row + skip)
        across = (((1,), (1,)), ((), ()))
        plain = jnp.dot(feats[group], here, preferred_element_type=jnp.float32)
        flipped = lax.dot_general(here_t, feats[group], across, preferred_element_type=jnp.float32)
        if skip + width > 128:
            plain += jnp.dot(feats[group + 1], there, preferred_element_type=jnp.float32)
            flipped += lax.dot_general(
                there_t, feats[group + 1], across, preferred_element_type=jnp.float32
            )
        return plain.astype(jnp.bfloat16), flipped.astype(jnp.bfloat16)

    base = 0
    for cos_start, sin_start, length in order_slices(LMAX, NBIN):
        count = length // NBIN
        parts = -(-length // 128)
        for kind_start in (cos_start, sin_start):
            if kind_start < 0:
                continue
            tiles = [
                aligned(kind_start + 128 * part, min(128, length - 128 * part))
                for part in range(parts)
            ]
            for up in range(parts):
                for over in range(parts):
                    product = jnp.dot(
                        tiles[up][1], tiles[over][0], preferred_element_type=jnp.float32
                    )
                    at = (over, slice(up * 128, up * 128 + 128))
                    if kind_start == cos_start:
                        gram[at] = product
                    else:
                        gram[at] += product
        lane = lax.broadcasted_iota(jnp.int32, (2 * count, 128), 1)
        for rest in range(8):
            for part in range(parts):
                units = min(8, count - 8 * part)
                shift = rest * count % 8
                at = base + rest * count // 8 + part
                value = gram[part, pl.ds(rest, 2 * count, stride=8), :] * (1.0 / PRIM_DEV)
                if shift:
                    value = pltpu.roll(value, 16 * shift, 1)
                window = pl.ds(at, 2 * count, stride=count)
                keep = (lane >= 16 * shift) & (lane < 16 * (shift + units))
                out_ref[window, :] = jnp.where(keep, value, out_ref[window, :])
                if shift + units > 8:
                    window = pl.ds(at + 1, 2 * count, stride=count)
                    keep = lane < 16 * (shift + units - 8)
                    out_ref[window, :] = jnp.where(keep, value, out_ref[window, :])
        base += 2 * count * count


def gram_rows(rows):
    total = sum(length * length for _, _, length in order_slices(LMAX, NBIN))
    return pl.pallas_call(
        gram_kernel,
        out_shape=jax.ShapeDtypeStruct((total // 128, 128), jnp.float32),
        in_specs=[pl.BlockSpec(memory_space=pltpu.VMEM)],
        out_specs=pl.BlockSpec(memory_space=pltpu.VMEM),
        scratch_shapes=[
            pltpu.VMEM((16, rows.shape[0], 128), jnp.bfloat16),
            pltpu.VMEM((2, 256, 128), jnp.float32),
        ],
        compiler_params=pltpu.CompilerParams(vmem_limit_bytes=40 << 20),
        name="gram_rows",
    )(rows)


def shards(prim_pos, prim_weight, sec_pos, sec_weight, sec_counts, tile_lists, region_of):
    box_count = lax.axis_size("box")
    help_count = lax.axis_size("help")
    per_device = sec_pos.shape[0]
    lane_index = jnp.arange(sec_pos.shape[2], dtype=jnp.int32)
    live_mask = (lane_index[None, :] < sec_counts[:, None]).astype(jnp.float32)
    count_row = jnp.broadcast_to(
        sec_counts.astype(jnp.float32)[:, None, None], (per_device, 4, sec_pos.shape[2])
    )
    own_blocks = jnp.concatenate(
        [sec_pos, (sec_weight * live_mask)[:, None, :], count_row], axis=1
    )
    chip_pool = lax.all_gather(own_blocks, "help", axis=0, tiled=True)
    block_pool = padded(chip_pool, (("box", 0),), chip_pool.shape[0])
    pool_counts = block_pool[:, 4, 0].astype(jnp.int32)
    in_use = tile_lists >= 0
    safe_list = jnp.where(in_use, tile_lists, 0)
    owner_dev = safe_list // per_device
    box_move = jnp.mod(owner_dev // help_count - lax.axis_index("box") + 1, box_count)
    pool_index = (
        box_move * (help_count * per_device)
        + owner_dev % help_count * per_device
        + safe_list % per_device
    )
    pool_index = jnp.where(in_use, pool_index, -1).astype(jnp.int32)
    row_total = prim_pos.shape[1]
    norm_scale = 1.0 / math.sqrt(LIST * BS)
    prim = jnp.concatenate([prim_pos, (prim_weight * norm_scale)[None, :]], axis=0).T

    coefficients, rows = pair_sums(pool_index, pool_counts, block_pool, prim)
    owner_rows = exchange(row_table(region_of[:, 0]), rows).reshape(-1, 16, 128)
    region_tensor = gram_rows(owner_rows).reshape(1, -1)
    return (coefficients, region_tensor)


def solution(mesh):
    placed = (
        P(None, ("box", "help")),
        P(("box", "help")),
        P(("box", "help"), None, None),
        P(("box", "help"), None),
        P(("box", "help")),
        P(("box", "help"), None),
        P(("box", "help"), None),
    )
    return jax.shard_map(
        shards,
        mesh=mesh,
        in_specs=placed,
        out_specs=(P(("box", "help"), None), P(("box", "help"), None)),
        check_vma=False,
    )
```

```python
import functools
import math

import jax
import jax.numpy as jnp
from jax import lax
from jax.experimental import pallas as pl
from jax.experimental.pallas import tpu as pltpu
from jax.sharding import PartitionSpec as P

LMAX = 10
NBIN = 16
BS = 128
LIST = 12
PT = 16
PRIM_DEV = 64
NHARM = (LMAX + 1) ** 2
FEAT = NHARM * NBIN
BOXES = 128
BLK_DEV = 8
Z_SIZE = 8
PLANE = 16
SOURCE_MOVES = (0, -1, 1, -2, 2, -3, 3, 4)
PEERS = 2 * PLANE
MESH = pl.DeviceIdType.MESH

GROUPS = ((0, 1), (2, 3), (4, 5, 6), (7, 8, 9, 10))


def order_slices(degree_top, bin_count):
    slices = []
    position = 0
    for m_order in range(degree_top + 1):
        length = (degree_top + 1 - m_order) * bin_count
        if m_order == 0:
            slices.append((position, -1, length))
            position = position + length
        else:
            slices.append((position, position + length, length))
            position = position + 2 * length
    return slices


def harmonic_scale(m_order, degree):
    factor = math.sqrt(
        (2 * degree + 1)
        / (4.0 * math.pi)
        * math.factorial(degree - m_order)
        / math.factorial(degree + m_order)
    )
    if m_order > 0:
        factor = factor * math.sqrt(2.0)
    lead = 1.0
    for odd_value in range(1, 2 * m_order, 2):
        lead = lead * odd_value
    for step in range(m_order + 1, degree + 1):
        lead = lead * (2 * step - 1) / (step - m_order)
    return factor * lead


def first_row(m_order):
    return order_slices(LMAX, 1)[m_order][0]


def near_kernel(counts_ref, pos_ref, weight_ref, region_ref, pool_ref, live_ref, code_ref, send, recv):
    box, core = lax.axis_index("box"), lax.axis_index("help")
    z_at, other = box // PLANE, 1 - core
    above, below = (box + 1) % BOXES, (box + BOXES - 1) % BOXES
    near = ((above, 0, 0), (above, 1, 0), (below, 0, 2), (below, 1, 2), (box, other, 1))
    line = [((z_at + step) % Z_SIZE * PLANE + box % PLANE, core) for step in range(1, Z_SIZE)]
    barrier = pltpu.get_barrier_semaphore()
    for to_box, to_core, _ in near:
        pl.semaphore_signal(barrier, inc=1, device_id=(to_box, to_core), device_id_type=MESH)
    for target in line:
        pl.semaphore_signal(barrier, inc=1, device_id=target, device_id_type=MESH)

    lane = lax.broadcasted_iota(jnp.int32, (1, BS), 1)
    mine = 2 + core
    live = jnp.zeros((1, BS), jnp.int32)
    for block in range(BLK_DEV):
        count = counts_ref[block]
        live = jnp.where(lane == block, count, live)
        for axis in range(3):
            pool_ref[mine, block, axis : axis + 1, :] = pos_ref[axis, block : block + 1, :]
        pool_ref[mine, block, 3:4, :] = jnp.where(lane < count, weight_ref[block : block + 1, :], 0.0)
        pool_ref[mine, block, 4:8, :] = jnp.zeros((4, BS), jnp.float32)
    live_ref[mine] = live
    row = lax.broadcasted_iota(jnp.int32, (PRIM_DEV, BS), 0)
    col = lax.broadcasted_iota(jnp.int32, (PRIM_DEV, BS), 1)
    over = jnp.concatenate([region_ref[...], jnp.zeros((1, BS - PRIM_DEV), jnp.int32)], axis=1)
    down = jnp.sum(jnp.where(row == col, over, 0), axis=1, keepdims=True)
    rank = jnp.sum(jnp.where((down == over) & (row < col), 1, 0), axis=0, keepdims=True)
    code_ref[z_at] = jnp.where(lane < PRIM_DEV, 2 * over + rank, -1)

    pl.semaphore_wait(barrier, 12)

    def block_copy(slot, kind, target):
        ref = (pool_ref, live_ref)[kind]
        return pltpu.make_async_remote_copy(
            src_ref=ref.at[mine],
            dst_ref=ref.at[slot],
            send_sem=send.at[slot, kind],
            recv_sem=recv.at[slot, kind],
            device_id=target,
            device_id_type=MESH,
        )

    def code_copy(z_from, step):
        return pltpu.make_async_remote_copy(
            src_ref=code_ref.at[z_from],
            dst_ref=code_ref.at[z_from],
            send_sem=send.at[5 + step, 0],
            recv_sem=recv.at[6 + z_from, 0],
            device_id=line[step - 1],
            device_id_type=MESH,
        )

    sends = []
    for at, (to_box, to_core, move) in enumerate(near):
        for kind in range(2):
            ref = (pool_ref, live_ref)[kind]
            sends.append(
                pltpu.make_async_remote_copy(
                    src_ref=ref.at[mine],
                    dst_ref=ref.at[2 * move + core],
                    send_sem=send.at[at, kind],
                    recv_sem=recv.at[2 * move + core, kind],
                    device_id=(to_box, to_core),
                    device_id_type=MESH,
                )
            )
    for step in range(1, Z_SIZE):
        sends.append(code_copy(z_at, step))
    for copy in sends:
        copy.start()
    for slot in (0, 1, 4, 5, 2 + other):
        for kind in range(2):
            block_copy(slot, kind, (box, other)).wait_recv()
    for step in range(1, Z_SIZE):
        code_copy((z_at + step) % Z_SIZE, step).wait_recv()
    for copy in sends:
        copy.wait_send()


def near(counts, pos, weight, regions):
    return pl.pallas_call(
        near_kernel,
        out_shape=(
            jax.ShapeDtypeStruct((6, BLK_DEV, 8, BS), jnp.float32),
            jax.ShapeDtypeStruct((6, 1, BS), jnp.int32),
            jax.ShapeDtypeStruct((Z_SIZE, 1, BS), jnp.int32),
        ),
        in_specs=[pl.BlockSpec(memory_space=pltpu.SMEM)]
        + [pl.BlockSpec(memory_space=pltpu.VMEM)] * 3,
        out_specs=(pl.BlockSpec(memory_space=pltpu.VMEM),) * 3,
        scratch_shapes=[pltpu.SemaphoreType.DMA((13, 2)), pltpu.SemaphoreType.DMA((14, 2))],
        compiler_params=pltpu.CompilerParams(collective_id=0, has_side_effects=True),
        name="near",
    )(counts, pos, weight, regions)


def turn_matrix():
    row = lax.broadcasted_iota(jnp.int32, (256, 256), 0)
    col = lax.broadcasted_iota(jnp.int32, (256, 256), 1)
    return jnp.where(col == (row % 16) * 16 + row // 16, 1.0, 0.0).astype(jnp.bfloat16)


def pair_kernel(
    list_ref, pool_ref, live_ref, code_ref, pos_ref, weight_ref, coef_ref, rows_ref, table_ref,
    packed, basis, spline, acc, diag, spread, live, sem
):
    tile = pl.program_id(0)
    box, core = lax.axis_index("box"), lax.axis_index("help")
    lane = lax.broadcasted_iota(jnp.int32, (8, BS), 1)

    @pl.when(tile == 0)
    def _():
        fetch = pltpu.make_async_copy(live_ref, live, sem)
        fetch.start()
        row = lax.broadcasted_iota(jnp.int32, (PT * NBIN, 128), 0)
        col = lax.broadcasted_iota(jnp.int32, (PT * NBIN, 128), 1)
        for part in range(8):
            spread[part] = jnp.where(col == part * NBIN + row // PT, 1.0, 0.0).astype(jnp.bfloat16)
        turn = lax.broadcasted_iota(jnp.int32, (2 * PEERS, BS), 0)
        over = lax.broadcasted_iota(jnp.int32, (2 * PEERS, BS), 1)
        x_to, y_to = (box // 4 + turn // 16) % 4, (box + turn // 4) % 4
        owner = (box // PLANE * PLANE + x_to * 4 + y_to) * 2 + (core + turn // 2) % 2
        wanted = owner * 2 + turn % 2
        table = jnp.zeros((2 * PEERS, BS), jnp.int32)
        for z_from in range(Z_SIZE):
            found = jnp.max(
                jnp.where(code_ref[z_from] == wanted, over, -1), axis=1, keepdims=True
            )
            table = jnp.where(over == z_from, found, table)
        table_ref[...] = table
        fetch.wait()

    packed[...] = jnp.zeros_like(packed)
    filled = jnp.int32(0)
    for slot in range(LIST):
        listed = list_ref[tile, slot]
        used = listed >= 0
        listed = jnp.maximum(listed, 0)
        owner = listed // BLK_DEV
        place = jnp.where(used, (owner // 2 - box + 1 + BOXES) % BOXES * 2 + owner % 2, 0)
        block = pool_ref[place, listed % BLK_DEV]
        base = filled // BS
        shift = filled % BS
        moved = pltpu.roll(block, shift, 1)
        low = jnp.where((lane >= shift) & used, moved, packed[base])
        packed[base] = low
        high = jnp.where((lane < shift) & used, moved, packed[base + 1])
        packed[base + 1] = high
        filled = filled + jnp.where(used, live[place, 0, listed % BLK_DEV], 0)
    chunks = (filled + 2 * BS - 1) // (2 * BS)

    acc[...] = jnp.zeros_like(acc)
    own = lax.broadcasted_iota(jnp.int32, (PT, PRIM_DEV), 0) + tile * PT
    own = own == lax.broadcasted_iota(jnp.int32, (PT, PRIM_DEV), 1)

    def column(values):
        return jnp.sum(jnp.where(own, values, 0.0), axis=1, keepdims=True)

    px, py, pz = [column(pos_ref[axis : axis + 1, :]) for axis in range(3)]
    scale_column = column(weight_ref[...]) * (1.0 / math.sqrt(LIST * BS))
    bin_step = 1.0 / (NBIN + 1)

    def chunk_step(chunk, carry):
        geometry = []
        for half in range(2):
            rows = packed[2 * chunk + half]
            dx = rows[0:1, :] - px
            dy = rows[1:2, :] - py
            dz = rows[2:3, :] - pz
            weight = jnp.broadcast_to(rows[3:4, :], (PT, BS))
            radius = jnp.sqrt(dx * dx + dy * dy + dz * dz)
            inverse = 1.0 / jnp.maximum(radius, 0.5 * bin_step)
            geometry.append((dx * inverse, dy * inverse, dz * inverse))
            place = radius * float(NBIN + 1)
            whole = jnp.floor(place)
            part = place - whole
            upper = weight * part
            lower = weight * (1.0 - part)
            cols = slice(half * BS, (half + 1) * BS)
            above = jnp.where(whole == 0.0, upper, 0.0)
            for bin_at in range(NBIN):
                here = whole == float(bin_at + 1)
                spline[bin_at * PT : (bin_at + 1) * PT, cols] = jnp.where(here, lower, above).astype(
                    jnp.bfloat16
                )
                above = jnp.where(here, upper, 0.0)
        angular = [[None, None], [None, None]]
        for orders in GROUPS:
            for half in range(2):
                ux, uy, uz = geometry[half]
                cols = slice(half * BS, (half + 1) * BS)
                for m_order in orders:
                    if m_order == 1:
                        angular[half] = [ux, uy]
                    elif m_order > 1:
                        cos_part, sin_part = angular[half]
                        angular[half] = [
                            cos_part * ux - sin_part * uy,
                            sin_part * ux + cos_part * uy,
                        ]
                    older, newer = None, None
                    start = first_row(m_order)
                    count = LMAX + 1 - m_order
                    for degree in range(m_order, LMAX + 1):
                        if degree == m_order:
                            current = None
                        elif degree == m_order + 1:
                            current = uz
                        else:
                            ratio = (degree + m_order - 1) * (degree - m_order - 1) / (
                                (2 * degree - 1) * (2 * degree - 3)
                            )
                            if older is None:
                                current = uz * newer - ratio
                            else:
                                current = uz * newer - ratio * older
                        older, newer = newer, current
                        scale = harmonic_scale(m_order, degree)
                        at = (start + degree - m_order) * PT
                        if current is None:
                            scaled = None
                        else:
                            scaled = current * scale
                        if m_order == 0:
                            value = jnp.full((PT, BS), scale, jnp.float32) if scaled is None else scaled
                            basis[at : at + PT, cols] = value.astype(jnp.bfloat16)
                        else:
                            for kind in range(2):
                                turn = angular[half][kind]
                                value = turn * scale if scaled is None else scaled * turn
                                low = at + kind * count * PT
                                basis[low : low + PT, cols] = value.astype(jnp.bfloat16)
            first = first_row(orders[0]) * PT
            last = NHARM * PT if orders[-1] == LMAX else first_row(orders[-1] + 1) * PT
            acc[first:last, :] += lax.dot_general(
                basis[first:last, :],
                spline[...],
                (((1,), (1,)), ((), ())),
                preferred_element_type=jnp.float32,
            )
        return carry

    lax.fori_loop(0, chunks, chunk_step, 0)

    row = lax.broadcasted_iota(jnp.int32, (PT, PT * NBIN), 0)
    col = lax.broadcasted_iota(jnp.int32, (PT, PT * NBIN), 1)
    keep = jnp.where(col % PT == row, scale_column, 0.0)
    for harm in range(128):
        if harm < NHARM:
            value = (acc[harm * PT : (harm + 1) * PT, :] * keep).astype(jnp.bfloat16)
        else:
            value = jnp.zeros((PT, PT * NBIN), jnp.bfloat16)
        diag[harm % 8, (harm // 8) * PT : (harm // 8 + 1) * PT, :] = value
    total = jnp.zeros((256, 128), jnp.float32)
    for part in range(8):
        total = total + jnp.dot(diag[part], spread[part], preferred_element_type=jnp.float32)
    rows = total.astype(jnp.bfloat16)
    for group in range(15):
        coef_ref[:, group * 128 : (group + 1) * 128] = rows[group * PT : (group + 1) * PT, :]
    coef_ref[:, 1920:FEAT] = rows[15 * PT : 16 * PT, : FEAT - 1920]
    turned = jnp.dot(turn_matrix(), rows, preferred_element_type=jnp.float32)
    rows_ref[...] = turned.astype(jnp.bfloat16).reshape(PT, 16, 128)


def pair_sums(lists, pool, live, codes, pos, weight):
    tiles = lists.shape[0]
    whole = pl.BlockSpec(memory_space=pltpu.VMEM)
    return pl.pallas_call(
        pair_kernel,
        out_shape=(
            jax.ShapeDtypeStruct((tiles * PT, FEAT), jnp.bfloat16),
            jax.ShapeDtypeStruct((tiles * PT, 16, 128), jnp.bfloat16),
            jax.ShapeDtypeStruct((2 * PEERS, BS), jnp.int32),
        ),
        grid_spec=pltpu.PrefetchScalarGridSpec(
            num_scalar_prefetch=1,
            grid=(tiles,),
            in_specs=[whole, pl.BlockSpec(memory_space=pl.ANY), whole, whole, whole],
            out_specs=(
                pl.BlockSpec((PT, FEAT), lambda t, *_: (t, 0)),
                pl.BlockSpec((PT, 16, 128), lambda t, *_: (t, 0, 0)),
                pl.BlockSpec((2 * PEERS, BS), lambda t, *_: (0, 0)),
            ),
            scratch_shapes=[
                pltpu.VMEM((2 * ((LIST + 1) // 2) + 2, 8, BS), jnp.float32),
                pltpu.VMEM((NHARM * PT, 2 * BS), jnp.bfloat16),
                pltpu.VMEM((NBIN * PT, 2 * BS), jnp.bfloat16),
                pltpu.VMEM((NHARM * PT, NBIN * PT), jnp.float32),
                pltpu.VMEM((8, 256, NBIN * PT), jnp.bfloat16),
                pltpu.VMEM((8, NBIN * PT, 128), jnp.bfloat16),
                pltpu.SMEM((6, 1, BS), jnp.int32),
                pltpu.SemaphoreType.DMA(()),
            ],
        ),
        compiler_params=pltpu.CompilerParams(vmem_limit_bytes=40 << 20),
        name="pair_sums",
    )(lists, pool, live, codes, pos, weight)


def exchange_kernel(table_ref, rows_ref, out_ref, *scratch):
    held = (rows_ref,) + scratch[:7]
    stage, ring_send, ring_recv, plane_send, plane_recv = scratch[7:]
    box, core = lax.axis_index("box"), lax.axis_index("help")
    z_at, x_at, y_at = box // PLANE, (box // 4) % 4, box % 4
    ring = (
        ((z_at + 1) % Z_SIZE * PLANE + box % PLANE, core),
        ((z_at + Z_SIZE - 1) % Z_SIZE * PLANE + box % PLANE, core),
    )

    def peer(turn):
        x_to, y_to = (x_at + turn // 8) % 4, (y_at + turn // 2 % 4) % 4
        return (z_at * PLANE + x_to * 4 + y_to, (core + turn % 2) % 2)

    barrier = pltpu.get_barrier_semaphore()
    for way in range(2):
        pl.semaphore_signal(barrier, inc=1, device_id=ring[way], device_id_type=MESH)

    def greet(turn, carry):
        pl.semaphore_signal(barrier, inc=1, device_id=peer(turn), device_id_type=MESH)
        return carry

    lax.fori_loop(1, PEERS, greet, 0)
    pl.semaphore_wait(barrier, PEERS + 1)

    def ring_copy(way, step, half):
        from_at = 0 if step == 1 else 2 * (step - 1) - 1 + way
        to_at = 7 if step == 4 else 2 * step - 1 + way
        part = pl.ds(half * (PRIM_DEV // 2), PRIM_DEV // 2)
        return pltpu.make_async_remote_copy(
            src_ref=held[from_at].at[part],
            dst_ref=held[to_at].at[part],
            send_sem=ring_send.at[way, step - 1, half],
            recv_sem=ring_recv.at[way, step - 1, half],
            device_id=ring[way],
            device_id_type=MESH,
        )

    def deal(batch, first, number):
        def fill(turn, target):
            for source in range(first, first + number):
                z_from = (z_at + SOURCE_MOVES[source] + Z_SIZE) % Z_SIZE
                for slot in range(2):
                    row = table_ref[turn * 2 + slot, z_from]
                    value = held[source][jnp.maximum(row, 0)]
                    target[turn, source, slot] = jnp.where(row >= 0, value, jnp.zeros_like(value))

        fill(0, out_ref)

        def one_peer(count, carry):
            turn = count * 13 % PEERS
            fill(turn, stage)
            pltpu.make_async_remote_copy(
                src_ref=stage.at[turn, pl.ds(first, number)],
                dst_ref=out_ref.at[turn, pl.ds(first, number)],
                send_sem=plane_send.at[batch],
                recv_sem=plane_recv.at[batch],
                device_id=peer(turn),
                device_id_type=MESH,
            ).start()
            return carry

        lax.fori_loop(1, PEERS, one_peer, 0)

    for half in range(2):
        for way in range(2):
            ring_copy(way, 1, half).start()
    deal(0, 0, 1)
    for step in range(1, 4):
        for half in range(2):
            for way in range(2):
                ring_copy(way, step, half).wait_recv()
                if step < 3 or half == way:
                    ring_copy(way, step + 1, half).start()
        deal(step, 2 * step - 1, 2)
    for way in range(2):
        ring_copy(way, 4, way).wait_recv()
    deal(4, 7, 1)
    for step in range(1, 5):
        for half in range(2):
            for way in range(2):
                if step < 4 or half == way:
                    ring_copy(way, step, half).wait_send()
    for batch, first, number in ((0, 0, 1), (1, 1, 2), (2, 3, 2), (3, 5, 2), (4, 7, 1)):
        sent = stage.at[pl.ds(1, PEERS - 1), pl.ds(first, number)]
        pltpu.make_async_copy(sent, sent, plane_send.at[batch]).wait()
        come = out_ref.at[pl.ds(1, PEERS - 1), pl.ds(first, number)]
        pltpu.make_async_copy(come, come, plane_recv.at[batch]).wait()


def exchange(table, rows):
    shape = (PEERS, Z_SIZE, 2, 16, 128)
    return pl.pallas_call(
        exchange_kernel,
        out_shape=jax.ShapeDtypeStruct(shape, rows.dtype),
        in_specs=[
            pl.BlockSpec(memory_space=pltpu.SMEM),
            pl.BlockSpec(memory_space=pltpu.VMEM),
        ],
        out_specs=pl.BlockSpec(memory_space=pltpu.VMEM),
        scratch_shapes=[pltpu.VMEM(rows.shape, rows.dtype)] * 7
        + [
            pltpu.VMEM(shape, rows.dtype),
            pltpu.SemaphoreType.DMA((2, 4, 2)),
            pltpu.SemaphoreType.DMA((2, 4, 2)),
            pltpu.SemaphoreType.DMA((5,)),
            pltpu.SemaphoreType.DMA((5,)),
        ],
        compiler_params=pltpu.CompilerParams(
            collective_id=1, has_side_effects=True, vmem_limit_bytes=40 << 20
        ),
        name="exchange",
    )(table, rows)


def gram_kernel(rows_ref, out_ref, feats, gram):
    row_total = rows_ref.shape[0]
    turn = turn_matrix()

    def regroup(step, carry):
        at = pl.multiple_of(step * 16, 16)
        block = rows_ref[pl.ds(at, 16)].reshape(256, 128)
        moved = jnp.dot(turn, block, preferred_element_type=jnp.float32).astype(jnp.bfloat16)
        feats[:, pl.ds(at, 16), :] = moved.reshape(16, 16, 128)
        return carry

    lax.fori_loop(0, row_total // 16, regroup, 0)
    row = lax.broadcasted_iota(jnp.int32, (128, 128), 0)
    col = lax.broadcasted_iota(jnp.int32, (128, 128), 1)

    def one_hot(cond):
        return jnp.where(cond, 1.0, 0.0).astype(jnp.bfloat16)

    def aligned(start, width):
        group, skip = start // 128, start % 128
        here, there = one_hot(row == col + skip), one_hot(row + 128 == col + skip)
        here_t, there_t = one_hot(col == row + skip), one_hot(col + 128 == row + skip)
        across = (((1,), (1,)), ((), ()))
        plain = jnp.dot(feats[group], here, preferred_element_type=jnp.float32)
        flipped = lax.dot_general(here_t, feats[group], across, preferred_element_type=jnp.float32)
        if skip + width > 128:
            plain += jnp.dot(feats[group + 1], there, preferred_element_type=jnp.float32)
            flipped += lax.dot_general(
                there_t, feats[group + 1], across, preferred_element_type=jnp.float32
            )
        return plain.astype(jnp.bfloat16), flipped.astype(jnp.bfloat16)

    base = 0
    for cos_start, sin_start, length in order_slices(LMAX, NBIN):
        count = length // NBIN
        parts = -(-length // 128)
        for kind_start in (cos_start, sin_start):
            if kind_start < 0:
                continue
            tiles = [
                aligned(kind_start + 128 * part, min(128, length - 128 * part))
                for part in range(parts)
            ]
            for up in range(parts):
                for over in range(parts):
                    product = jnp.dot(
                        tiles[up][1], tiles[over][0], preferred_element_type=jnp.float32
                    )
                    at = (over, slice(up * 128, up * 128 + 128))
                    if kind_start == cos_start:
                        gram[at] = product
                    else:
                        gram[at] += product
        lane = lax.broadcasted_iota(jnp.int32, (2 * count, 128), 1)
        for rest in range(8):
            for part in range(parts):
                units = min(8, count - 8 * part)
                shift = rest * count % 8
                at = base + rest * count // 8 + part
                value = gram[part, pl.ds(rest, 2 * count, stride=8), :] * (1.0 / PRIM_DEV)
                if shift:
                    value = pltpu.roll(value, 16 * shift, 1)
                window = pl.ds(at, 2 * count, stride=count)
                keep = (lane >= 16 * shift) & (lane < 16 * (shift + units))
                out_ref[window, :] = jnp.where(keep, value, out_ref[window, :])
                if shift + units > 8:
                    window = pl.ds(at + 1, 2 * count, stride=count)
                    keep = lane < 16 * (shift + units - 8)
                    out_ref[window, :] = jnp.where(keep, value, out_ref[window, :])
        base += 2 * count * count


def gram_rows(rows):
    total = sum(length * length for _, _, length in order_slices(LMAX, NBIN))
    return pl.pallas_call(
        gram_kernel,
        out_shape=jax.ShapeDtypeStruct((total // 128, 128), jnp.float32),
        in_specs=[pl.BlockSpec(memory_space=pltpu.VMEM)],
        out_specs=pl.BlockSpec(memory_space=pltpu.VMEM),
        scratch_shapes=[
            pltpu.VMEM((16, rows.shape[0], 128), jnp.bfloat16),
            pltpu.VMEM((2, 256, 128), jnp.float32),
        ],
        compiler_params=pltpu.CompilerParams(vmem_limit_bytes=40 << 20),
        name="gram_rows",
    )(rows)


def shards(prim_pos, prim_weight, sec_pos, sec_weight, sec_counts, tile_lists, region_of):
    pool, live, codes = near(
        sec_counts, sec_pos.transpose(1, 0, 2), sec_weight, region_of.reshape(1, -1)
    )
    coefficients, rows, table = pair_sums(
        tile_lists, pool, live, codes, prim_pos, prim_weight.reshape(1, -1)
    )
    owner_rows = exchange(table, rows).reshape(-1, 16, 128)
    region_tensor = gram_rows(owner_rows).reshape(1, -1)
    return (coefficients, region_tensor)


def solution(mesh):
    placed = (
        P(None, ("box", "help")),
        P(("box", "help")),
        P(("box", "help"), None, None),
        P(("box", "help"), None),
        P(("box", "help")),
        P(("box", "help"), None),
        P(("box", "help"), None),
    )
    return jax.shard_map(
        shards,
        mesh=mesh,
        in_specs=placed,
        out_specs=(P(("box", "help"), None), P(("box", "help"), None)),
        check_vma=False,
    )
```

```python
import functools
import math

import jax
import jax.numpy as jnp
from jax import lax
from jax.experimental import pallas as pl
from jax.experimental.pallas import tpu as pltpu
from jax.sharding import PartitionSpec as P

LMAX = 10
NBIN = 16
BS = 128
LIST = 12
PT = 16
PRIM_DEV = 64
NHARM = (LMAX + 1) ** 2
FEAT = NHARM * NBIN
BOXES = 128
BLK_DEV = 8
Z_SIZE = 8
PLANE = 16
SOURCE_MOVES = (0, -1, 1, -2, 2, -3, 3, 4)
PEERS = 2 * PLANE
MESH = pl.DeviceIdType.MESH

GROUPS = ((0, 1), (2, 3), (4, 5, 6), (7, 8, 9, 10))


def order_slices(degree_top, bin_count):
    slices = []
    position = 0
    for m_order in range(degree_top + 1):
        length = (degree_top + 1 - m_order) * bin_count
        if m_order == 0:
            slices.append((position, -1, length))
            position = position + length
        else:
            slices.append((position, position + length, length))
            position = position + 2 * length
    return slices


def harmonic_scale(m_order, degree):
    factor = math.sqrt(
        (2 * degree + 1)
        / (4.0 * math.pi)
        * math.factorial(degree - m_order)
        / math.factorial(degree + m_order)
    )
    if m_order > 0:
        factor = factor * math.sqrt(2.0)
    lead = 1.0
    for odd_value in range(1, 2 * m_order, 2):
        lead = lead * odd_value
    for step in range(m_order + 1, degree + 1):
        lead = lead * (2 * step - 1) / (step - m_order)
    return factor * lead


def first_row(m_order):
    return order_slices(LMAX, 1)[m_order][0]


def near_kernel(counts_ref, pos_ref, weight_ref, region_ref, pool_ref, live_ref, code_ref, send, recv):
    box, core = lax.axis_index("box"), lax.axis_index("help")
    z_at, other = box // PLANE, 1 - core
    above, below = (box + 1) % BOXES, (box + BOXES - 1) % BOXES
    near = ((above, 0, 0), (above, 1, 0), (below, 0, 2), (below, 1, 2), (box, other, 1))
    line = [((z_at + step) % Z_SIZE * PLANE + box % PLANE, core) for step in range(1, Z_SIZE)]
    barrier = pltpu.get_barrier_semaphore()
    for to_box, to_core, _ in near:
        pl.semaphore_signal(barrier, inc=1, device_id=(to_box, to_core), device_id_type=MESH)
    for target in line:
        pl.semaphore_signal(barrier, inc=1, device_id=target, device_id_type=MESH)

    lane = lax.broadcasted_iota(jnp.int32, (1, BS), 1)
    mine = 2 + core
    live = jnp.zeros((1, BS), jnp.int32)
    for block in range(BLK_DEV):
        count = counts_ref[block]
        live = jnp.where(lane == block, count, live)
        for axis in range(3):
            pool_ref[mine, block, axis : axis + 1, :] = pos_ref[axis, block : block + 1, :]
        pool_ref[mine, block, 3:4, :] = jnp.where(lane < count, weight_ref[block : block + 1, :], 0.0)
        pool_ref[mine, block, 4:8, :] = jnp.zeros((4, BS), jnp.float32)
    live_ref[mine] = live
    row = lax.broadcasted_iota(jnp.int32, (PRIM_DEV, BS), 0)
    col = lax.broadcasted_iota(jnp.int32, (PRIM_DEV, BS), 1)
    over = jnp.concatenate([region_ref[...], jnp.zeros((1, BS - PRIM_DEV), jnp.int32)], axis=1)
    down = jnp.sum(jnp.where(row == col, over, 0), axis=1, keepdims=True)
    rank = jnp.sum(jnp.where((down == over) & (row < col), 1, 0), axis=0, keepdims=True)
    code_ref[z_at] = jnp.where(lane < PRIM_DEV, 2 * over + rank, -1)

    pl.semaphore_wait(barrier, 12)

    def block_copy(slot, kind, target):
        ref = (pool_ref, live_ref)[kind]
        return pltpu.make_async_remote_copy(
            src_ref=ref.at[mine],
            dst_ref=ref.at[slot],
            send_sem=send.at[slot, kind],
            recv_sem=recv.at[slot, kind],
            device_id=target,
            device_id_type=MESH,
        )

    def code_copy(z_from, step):
        return pltpu.make_async_remote_copy(
            src_ref=code_ref.at[z_from],
            dst_ref=code_ref.at[z_from],
            send_sem=send.at[5 + step, 0],
            recv_sem=recv.at[6 + z_from, 0],
            device_id=line[step - 1],
            device_id_type=MESH,
        )

    sends = []
    for at, (to_box, to_core, move) in enumerate(near):
        for kind in range(2):
            ref = (pool_ref, live_ref)[kind]
            sends.append(
                pltpu.make_async_remote_copy(
                    src_ref=ref.at[mine],
                    dst_ref=ref.at[2 * move + core],
                    send_sem=send.at[at, kind],
                    recv_sem=recv.at[2 * move + core, kind],
                    device_id=(to_box, to_core),
                    device_id_type=MESH,
                )
            )
    for step in range(1, Z_SIZE):
        sends.append(code_copy(z_at, step))
    for copy in sends:
        copy.start()
    for slot in (0, 1, 4, 5, 2 + other):
        for kind in range(2):
            block_copy(slot, kind, (box, other)).wait_recv()
    for step in range(1, Z_SIZE):
        code_copy((z_at + step) % Z_SIZE, step).wait_recv()
    for copy in sends:
        copy.wait_send()


def near(counts, pos, weight, regions):
    return pl.pallas_call(
        near_kernel,
        out_shape=(
            jax.ShapeDtypeStruct((6, BLK_DEV, 8, BS), jnp.float32),
            jax.ShapeDtypeStruct((6, 1, BS), jnp.int32),
            jax.ShapeDtypeStruct((Z_SIZE, 1, BS), jnp.int32),
        ),
        in_specs=[pl.BlockSpec(memory_space=pltpu.SMEM)]
        + [pl.BlockSpec(memory_space=pltpu.VMEM)] * 3,
        out_specs=(pl.BlockSpec(memory_space=pltpu.VMEM),) * 3,
        scratch_shapes=[pltpu.SemaphoreType.DMA((13, 2)), pltpu.SemaphoreType.DMA((14, 2))],
        compiler_params=pltpu.CompilerParams(
            collective_id=0, has_side_effects=True, vmem_limit_bytes=8 << 20
        ),
        name="near",
    )(counts, pos, weight, regions)


def turn_matrix():
    row = lax.broadcasted_iota(jnp.int32, (256, 256), 0)
    col = lax.broadcasted_iota(jnp.int32, (256, 256), 1)
    return jnp.where(col == (row % 16) * 16 + row // 16, 1.0, 0.0).astype(jnp.bfloat16)


def pair_kernel(
    list_ref, pool_hbm, live_hbm, code_hbm, pos_hbm, weight_hbm, coef_ref, rows_ref, table_ref,
    packed, basis, spline, acc, diag, spread, pool_ref, live, code_ref, pos_ref, weight_ref, sem
):
    tile = pl.program_id(0)
    box, core = lax.axis_index("box"), lax.axis_index("help")
    lane = lax.broadcasted_iota(jnp.int32, (8, BS), 1)

    @pl.when(tile == 0)
    def _():
        fetches = [
            pltpu.make_async_copy(source, target, sem.at[at])
            for at, (source, target) in enumerate(
                (
                    (pool_hbm, pool_ref),
                    (live_hbm, live),
                    (code_hbm, code_ref),
                    (pos_hbm, pos_ref),
                    (weight_hbm, weight_ref),
                )
            )
        ]
        for fetch in fetches:
            fetch.start()
        row = lax.broadcasted_iota(jnp.int32, (PT * NBIN, 128), 0)
        col = lax.broadcasted_iota(jnp.int32, (PT * NBIN, 128), 1)
        for part in range(8):
            spread[part] = jnp.where(col == part * NBIN + row // PT, 1.0, 0.0).astype(jnp.bfloat16)
        for fetch in fetches:
            fetch.wait()
        turn = lax.broadcasted_iota(jnp.int32, (2 * PEERS, BS), 0)
        over = lax.broadcasted_iota(jnp.int32, (2 * PEERS, BS), 1)
        x_to, y_to = (box // 4 + turn // 16) % 4, (box + turn // 4) % 4
        owner = (box // PLANE * PLANE + x_to * 4 + y_to) * 2 + (core + turn // 2) % 2
        wanted = owner * 2 + turn % 2
        table = jnp.zeros((2 * PEERS, BS), jnp.int32)
        for z_from in range(Z_SIZE):
            found = jnp.max(
                jnp.where(code_ref[z_from] == wanted, over, -1), axis=1, keepdims=True
            )
            table = jnp.where(over == z_from, found, table)
        table_ref[...] = table

    packed[...] = jnp.zeros_like(packed)
    filled = jnp.int32(0)
    for slot in range(LIST):
        listed = list_ref[tile, slot]
        used = listed >= 0
        listed = jnp.maximum(listed, 0)
        owner = listed // BLK_DEV
        place = jnp.where(used, (owner // 2 - box + 1 + BOXES) % BOXES * 2 + owner % 2, 0)
        block = pool_ref[place, listed % BLK_DEV]
        base = filled // BS
        shift = filled % BS
        moved = pltpu.roll(block, shift, 1)
        low = jnp.where((lane >= shift) & used, moved, packed[base])
        packed[base] = low
        high = jnp.where((lane < shift) & used, moved, packed[base + 1])
        packed[base + 1] = high
        filled = filled + jnp.where(used, live[place, 0, listed % BLK_DEV], 0)
    chunks = (filled + 2 * BS - 1) // (2 * BS)

    acc[...] = jnp.zeros_like(acc)
    own = lax.broadcasted_iota(jnp.int32, (PT, PRIM_DEV), 0) + tile * PT
    own = own == lax.broadcasted_iota(jnp.int32, (PT, PRIM_DEV), 1)

    def column(values):
        return jnp.sum(jnp.where(own, values, 0.0), axis=1, keepdims=True)

    px, py, pz = [column(pos_ref[axis : axis + 1, :]) for axis in range(3)]
    scale_column = column(weight_ref[...]) * (1.0 / math.sqrt(LIST * BS))
    bin_step = 1.0 / (NBIN + 1)

    def chunk_step(chunk, carry):
        geometry = []
        for half in range(2):
            rows = packed[2 * chunk + half]
            dx = rows[0:1, :] - px
            dy = rows[1:2, :] - py
            dz = rows[2:3, :] - pz
            weight = jnp.broadcast_to(rows[3:4, :], (PT, BS))
            radius = jnp.sqrt(dx * dx + dy * dy + dz * dz)
            inverse = 1.0 / jnp.maximum(radius, 0.5 * bin_step)
            geometry.append((dx * inverse, dy * inverse, dz * inverse))
            place = radius * float(NBIN + 1)
            whole = jnp.floor(place)
            part = place - whole
            upper = weight * part
            lower = weight * (1.0 - part)
            cols = slice(half * BS, (half + 1) * BS)
            above = jnp.where(whole == 0.0, upper, 0.0)
            for bin_at in range(NBIN):
                here = whole == float(bin_at + 1)
                spline[bin_at * PT : (bin_at + 1) * PT, cols] = jnp.where(here, lower, above).astype(
                    jnp.bfloat16
                )
                above = jnp.where(here, upper, 0.0)
        angular = [[None, None], [None, None]]
        for orders in GROUPS:
            for half in range(2):
                ux, uy, uz = geometry[half]
                cols = slice(half * BS, (half + 1) * BS)
                for m_order in orders:
                    if m_order == 1:
                        angular[half] = [ux, uy]
                    elif m_order > 1:
                        cos_part, sin_part = angular[half]
                        angular[half] = [
                            cos_part * ux - sin_part * uy,
                            sin_part * ux + cos_part * uy,
                        ]
                    older, newer = None, None
                    start = first_row(m_order)
                    count = LMAX + 1 - m_order
                    for degree in range(m_order, LMAX + 1):
                        if degree == m_order:
                            current = None
                        elif degree == m_order + 1:
                            current = uz
                        else:
                            ratio = (degree + m_order - 1) * (degree - m_order - 1) / (
                                (2 * degree - 1) * (2 * degree - 3)
                            )
                            if older is None:
                                current = uz * newer - ratio
                            else:
                                current = uz * newer - ratio * older
                        older, newer = newer, current
                        scale = harmonic_scale(m_order, degree)
                        at = (start + degree - m_order) * PT
                        if current is None:
                            scaled = None
                        else:
                            scaled = current * scale
                        if m_order == 0:
                            value = jnp.full((PT, BS), scale, jnp.float32) if scaled is None else scaled
                            basis[at : at + PT, cols] = value.astype(jnp.bfloat16)
                        else:
                            for kind in range(2):
                                turn = angular[half][kind]
                                value = turn * scale if scaled is None else scaled * turn
                                low = at + kind * count * PT
                                basis[low : low + PT, cols] = value.astype(jnp.bfloat16)
            first = first_row(orders[0]) * PT
            last = NHARM * PT if orders[-1] == LMAX else first_row(orders[-1] + 1) * PT
            acc[first:last, :] += lax.dot_general(
                basis[first:last, :],
                spline[...],
                (((1,), (1,)), ((), ())),
                preferred_element_type=jnp.float32,
            )
        return carry

    lax.fori_loop(0, chunks, chunk_step, 0)

    row = lax.broadcasted_iota(jnp.int32, (PT, PT * NBIN), 0)
    col = lax.broadcasted_iota(jnp.int32, (PT, PT * NBIN), 1)
    keep = jnp.where(col % PT == row, scale_column, 0.0)
    for harm in range(128):
        if harm < NHARM:
            value = (acc[harm * PT : (harm + 1) * PT, :] * keep).astype(jnp.bfloat16)
        else:
            value = jnp.zeros((PT, PT * NBIN), jnp.bfloat16)
        diag[harm % 8, (harm // 8) * PT : (harm // 8 + 1) * PT, :] = value
    total = jnp.zeros((256, 128), jnp.float32)
    for part in range(8):
        total = total + jnp.dot(diag[part], spread[part], preferred_element_type=jnp.float32)
    rows = total.astype(jnp.bfloat16)
    for group in range(15):
        coef_ref[:, group * 128 : (group + 1) * 128] = rows[group * PT : (group + 1) * PT, :]
    coef_ref[:, 1920:FEAT] = rows[15 * PT : 16 * PT, : FEAT - 1920]
    turned = jnp.dot(turn_matrix(), rows, preferred_element_type=jnp.float32)
    rows_ref[...] = turned.astype(jnp.bfloat16).reshape(PT, 16, 128)


def pair_sums(lists, pool, live, codes, pos, weight):
    tiles = lists.shape[0]
    operands = (pool, live, codes, pos, weight)
    return pl.pallas_call(
        pair_kernel,
        out_shape=(
            jax.ShapeDtypeStruct((tiles * PT, FEAT), jnp.bfloat16),
            jax.ShapeDtypeStruct((tiles * PT, 16, 128), jnp.bfloat16),
            jax.ShapeDtypeStruct((2 * PEERS, BS), jnp.int32),
        ),
        grid_spec=pltpu.PrefetchScalarGridSpec(
            num_scalar_prefetch=1,
            grid=(tiles,),
            in_specs=[pl.BlockSpec(memory_space=pltpu.HBM)] * len(operands),
            out_specs=(
                pl.BlockSpec((PT, FEAT), lambda t, *_: (t, 0)),
                pl.BlockSpec((PT, 16, 128), lambda t, *_: (t, 0, 0)),
                pl.BlockSpec((2 * PEERS, BS), lambda t, *_: (0, 0)),
            ),
            scratch_shapes=[
                pltpu.VMEM((2 * ((LIST + 1) // 2) + 2, 8, BS), jnp.float32),
                pltpu.VMEM((NHARM * PT, 2 * BS), jnp.bfloat16),
                pltpu.VMEM((NBIN * PT, 2 * BS), jnp.bfloat16),
                pltpu.VMEM((NHARM * PT, NBIN * PT), jnp.float32),
                pltpu.VMEM((8, 256, NBIN * PT), jnp.bfloat16),
                pltpu.VMEM((8, NBIN * PT, 128), jnp.bfloat16),
                pltpu.VMEM(pool.shape, pool.dtype),
                pltpu.SMEM(live.shape, live.dtype),
                pltpu.VMEM(codes.shape, codes.dtype),
                pltpu.VMEM(pos.shape, pos.dtype),
                pltpu.VMEM(weight.shape, weight.dtype),
                pltpu.SemaphoreType.DMA((len(operands),)),
            ],
        ),
        compiler_params=pltpu.CompilerParams(vmem_limit_bytes=40 << 20),
        name="pair_sums",
    )(lists, *operands)


def gram_tiles():
    tiles = []
    for m_order, (cos_start, sin_start, length) in enumerate(order_slices(LMAX, NBIN)):
        for kind, start in enumerate((cos_start, sin_start)):
            if start >= 0:
                for part in range(-(-length // 128)):
                    width = min(128, length - 128 * part)
                    tiles.append((m_order, kind, start + 128 * part, width))
    return tiles


def gram_flatten(gram, out_ref, base, count):
    lane = lax.broadcasted_iota(jnp.int32, (2 * count, 128), 1)
    for rest in range(8):
        for part in range(-(-count // 8)):
            units = min(8, count - 8 * part)
            shift = rest * count % 8
            at = base + rest * count // 8 + part
            value = gram[part, pl.ds(rest, 2 * count, stride=8), :] * (1.0 / PRIM_DEV)
            if shift:
                value = pltpu.roll(value, 16 * shift, 1)
            window = pl.ds(at, 2 * count, stride=count)
            keep = (lane >= 16 * shift) & (lane < 16 * (shift + units))
            out_ref[window, :] = jnp.where(keep, value, out_ref[window, :])
            if shift + units > 8:
                window = pl.ds(at + 1, 2 * count, stride=count)
                keep = lane < 16 * (shift + units - 8)
                out_ref[window, :] = jnp.where(keep, value, out_ref[window, :])


PLANE_MOVES = (
    (1, 0), (3, 0), (0, 1), (0, 3), (1, 1), (3, 3), (1, 3), (3, 1),
    (2, 0), (0, 2), (2, 2), (2, 1), (1, 2), (2, 3), (3, 2),
)
BATCHES = ((0, 1), (1, 2), (3, 2), (5, 2), (7, 1))


def regions_kernel(table_ref, rows_ref, out_ref, *scratch):
    held = (rows_ref,) + scratch[:7]
    stage, come, feats, shifts, plain, flipped, gram = scratch[7:14]
    ring_send, ring_recv, plane_send, plane_recv = scratch[14:]
    box, core = lax.axis_index("box"), lax.axis_index("help")
    z_at, x_at, y_at = box // PLANE, (box // 4) % 4, box % 4
    ring = (
        ((z_at + 1) % Z_SIZE * PLANE + box % PLANE, core),
        ((z_at + Z_SIZE - 1) % Z_SIZE * PLANE + box % PLANE, core),
    )

    def peer(turn):
        x_to, y_to = (x_at + turn // 8) % 4, (y_at + turn // 2 % 4) % 4
        return (z_at * PLANE + x_to * 4 + y_to, (core + turn % 2) % 2)

    barrier = pltpu.get_barrier_semaphore()
    for way in range(2):
        pl.semaphore_signal(barrier, inc=1, device_id=ring[way], device_id_type=MESH)

    def greet(turn, carry):
        pl.semaphore_signal(barrier, inc=1, device_id=peer(turn), device_id_type=MESH)
        return carry

    lax.fori_loop(1, PEERS, greet, 0)
    pl.semaphore_wait(barrier, PEERS + 1)

    def ring_copy(way, step, half):
        from_at = 0 if step == 1 else 2 * (step - 1) - 1 + way
        to_at = 7 if step == 4 else 2 * step - 1 + way
        part = pl.ds(half * (PRIM_DEV // 2), PRIM_DEV // 2)
        return pltpu.make_async_remote_copy(
            src_ref=held[from_at].at[part],
            dst_ref=held[to_at].at[part],
            send_sem=ring_send.at[way, step - 1, half],
            recv_sem=ring_recv.at[way, step - 1, half],
            device_id=ring[way],
            device_id_type=MESH,
        )

    def deal(batch):
        first, number = BATCHES[batch]

        def fill(turn, target):
            for source in range(first, first + number):
                z_from = (z_at + SOURCE_MOVES[source] + Z_SIZE) % Z_SIZE
                for slot in range(2):
                    row = table_ref[turn * 2 + slot, z_from]
                    value = held[source][jnp.maximum(row, 0)]
                    target[turn, source, slot] = jnp.where(row >= 0, value, jnp.zeros_like(value))

        def one_peer(turn):
            fill(turn, stage)
            pltpu.make_async_remote_copy(
                src_ref=stage.at[turn, pl.ds(first, number)],
                dst_ref=come.at[turn, pl.ds(first, number)],
                send_sem=plane_send.at[batch],
                recv_sem=plane_recv.at[batch],
                device_id=peer(turn),
                device_id_type=MESH,
            ).start()

        def one_core(core_move, carry):
            for x_move, y_move in PLANE_MOVES:
                one_peer(x_move * 8 + y_move * 2 + core_move)
            return carry

        lax.fori_loop(0, 2, one_core, 0)
        one_peer(1)
        fill(0, come)

    tiles = gram_tiles()
    across = (((1,), (1,)), ((), ()))

    def prepare():
        row = lax.broadcasted_iota(jnp.int32, (128, 128), 0)
        col = lax.broadcasted_iota(jnp.int32, (128, 128), 1)
        for unit in range(-7, 8):
            hit = row == col + 16 * unit
            shifts[unit + 7] = jnp.where(hit, 1.0, 0.0).astype(jnp.bfloat16)

    def collect(batch):
        first, number = BATCHES[batch]
        arrived = come.at[pl.ds(1, PEERS - 1), pl.ds(first, number)]
        pltpu.make_async_copy(arrived, arrived, plane_recv.at[batch]).wait()
        turn = turn_matrix()
        for source in range(number):

            def regroup(step, carry, source=source):
                block = come[pl.ds(step * 8, 8), first + source].reshape(256, 128)
                moved = jnp.dot(turn, block, preferred_element_type=jnp.float32)
                at = pl.multiple_of(source * 64 + step * 16, 16)
                feats[:, pl.ds(at, 16), :] = moved.astype(jnp.bfloat16).reshape(16, 16, 128)
                return carry

            lax.fori_loop(0, 4, regroup, 0, unroll=True)
        size = 64 * number
        at = (384, 0, 128, 256, 448)[batch]
        for tile, (_, _, start, width) in enumerate(tiles):
            group, skip = start // 128, start % 128 // 16
            here = feats[group, 0:size, :]
            over = lax.dot_general(
                shifts[7 - skip], here, across, preferred_element_type=jnp.float32
            )
            if skip == 0:
                down = here
            else:
                down = jnp.dot(here, shifts[7 + skip], preferred_element_type=jnp.float32)
                if skip * 16 + width > 128:
                    there = feats[group + 1, 0:size, :]
                    down += jnp.dot(there, shifts[skip - 1], preferred_element_type=jnp.float32)
                    over += lax.dot_general(
                        shifts[15 - skip], there, across, preferred_element_type=jnp.float32
                    )
            plain[tile, at : at + size, :] = down.astype(jnp.bfloat16)
            flipped[tile, :, at : at + size] = over.astype(jnp.bfloat16)

    for half in range(2):
        for way in range(2):
            ring_copy(way, 1, half).start()
    deal(0)
    prepare()
    for step in range(1, 4):
        for half in range(2):
            for way in range(2):
                ring_copy(way, step, half).wait_recv()
                if step < 3 or half == way:
                    ring_copy(way, step + 1, half).start()
            if half == 0 and step > 1:
                collect(step - 2)
        deal(step)
    for way in range(2):
        ring_copy(way, 4, way).wait_recv()
    deal(4)
    for batch in range(2, 5):
        collect(batch)

    base = 0
    for m_order, (_, _, length) in enumerate(order_slices(LMAX, NBIN)):
        parts = -(-length // 128)
        for kind in range(2):
            mine = [at for at, tile in enumerate(tiles) if tile[:2] == (m_order, kind)]
            for up, up_tile in enumerate(mine):
                for over, over_tile in enumerate(mine):
                    product = jnp.dot(
                        flipped[up_tile], plain[over_tile], preferred_element_type=jnp.float32
                    )
                    at = (over, slice(up * 128, up * 128 + 128))
                    if kind == 0:
                        gram[at] = product
                    else:
                        gram[at] += product
        gram_flatten(gram, out_ref, base, length // NBIN)
        base += length * length // 128

    for step in range(1, 5):
        for half in range(2):
            for way in range(2):
                if step < 4 or half == way:
                    ring_copy(way, step, half).wait_send()
    for batch, (first, number) in enumerate(BATCHES):
        sent = stage.at[pl.ds(1, PEERS - 1), pl.ds(first, number)]
        pltpu.make_async_copy(sent, sent, plane_send.at[batch]).wait()


def region_products(table, rows):
    shape = (PEERS, Z_SIZE, 2, 16, 128)
    total = sum(length * length for _, _, length in order_slices(LMAX, NBIN))
    tiles = len(gram_tiles())
    row_total = PEERS * Z_SIZE * 2
    return pl.pallas_call(
        regions_kernel,
        out_shape=jax.ShapeDtypeStruct((total // 128, 128), jnp.float32),
        in_specs=[
            pl.BlockSpec(memory_space=pltpu.SMEM),
            pl.BlockSpec(memory_space=pltpu.VMEM),
        ],
        out_specs=pl.BlockSpec(memory_space=pltpu.VMEM),
        scratch_shapes=[pltpu.VMEM(rows.shape, rows.dtype)] * 7
        + [
            pltpu.VMEM(shape, rows.dtype),
            pltpu.VMEM(shape, rows.dtype),
            pltpu.VMEM((16, 128, 128), rows.dtype),
            pltpu.VMEM((15, 128, 128), rows.dtype),
            pltpu.VMEM((tiles, row_total, 128), rows.dtype),
            pltpu.VMEM((tiles, 128, row_total), rows.dtype),
            pltpu.VMEM((2, 256, 128), jnp.float32),
            pltpu.SemaphoreType.DMA((2, 4, 2)),
            pltpu.SemaphoreType.DMA((2, 4, 2)),
            pltpu.SemaphoreType.DMA((5,)),
            pltpu.SemaphoreType.DMA((5,)),
        ],
        compiler_params=pltpu.CompilerParams(
            collective_id=1, has_side_effects=True, vmem_limit_bytes=40 << 20
        ),
        name="region_products",
    )(table, rows)


def shards(prim_pos, prim_weight, sec_pos, sec_weight, sec_counts, tile_lists, region_of):
    pool, live, codes = near(
        sec_counts, sec_pos.transpose(1, 0, 2), sec_weight, region_of.reshape(1, -1)
    )
    coefficients, rows, table = pair_sums(
        tile_lists, pool, live, codes, prim_pos, prim_weight.reshape(1, -1)
    )
    region_tensor = region_products(table, rows).reshape(1, -1)
    return (coefficients, region_tensor)


def solution(mesh):
    placed = (
        P(None, ("box", "help")),
        P(("box", "help")),
        P(("box", "help"), None, None),
        P(("box", "help"), None),
        P(("box", "help")),
        P(("box", "help"), None),
        P(("box", "help"), None),
    )
    return jax.shard_map(
        shards,
        mesh=mesh,
        in_specs=placed,
        out_specs=(P(("box", "help"), None), P(("box", "help"), None)),
        check_vma=False,
    )
```

```python
import functools
import math

import jax
import jax.numpy as jnp
from jax import lax
from jax.experimental import pallas as pl
from jax.experimental.pallas import tpu as pltpu
from jax.sharding import PartitionSpec as P

LMAX = 10
NBIN = 16
BS = 128
LIST = 12
PT = 16
PRIM_DEV = 64
NHARM = (LMAX + 1) ** 2
FEAT = NHARM * NBIN
BOXES = 128
BLK_DEV = 8
Z_SIZE = 8
PLANE = 16
SOURCE_MOVES = (0, -1, 1, -2, 2, -3, 3, 4)
PEERS = 2 * PLANE
MESH = pl.DeviceIdType.MESH

GROUPS = ((0, 1, 2, 3, 4, 5, 6, 7, 8, 9, 10),)


def order_slices(degree_top, bin_count):
    slices = []
    position = 0
    for m_order in range(degree_top + 1):
        length = (degree_top + 1 - m_order) * bin_count
        if m_order == 0:
            slices.append((position, -1, length))
            position = position + length
        else:
            slices.append((position, position + length, length))
            position = position + 2 * length
    return slices


def harmonic_scale(m_order, degree):
    factor = math.sqrt(
        (2 * degree + 1)
        / (4.0 * math.pi)
        * math.factorial(degree - m_order)
        / math.factorial(degree + m_order)
    )
    if m_order > 0:
        factor = factor * math.sqrt(2.0)
    lead = 1.0
    for odd_value in range(1, 2 * m_order, 2):
        lead = lead * odd_value
    for step in range(m_order + 1, degree + 1):
        lead = lead * (2 * step - 1) / (step - m_order)
    return factor * lead


def first_row(m_order):
    return order_slices(LMAX, 1)[m_order][0]


def turn_matrix():
    row = lax.broadcasted_iota(jnp.int32, (256, 256), 0)
    col = lax.broadcasted_iota(jnp.int32, (256, 256), 1)
    return jnp.where(col == (row % 16) * 16 + row // 16, 1.0, 0.0).astype(jnp.bfloat16)


def near_kernel(
    counts_ref, pos_ref, weight_ref, region_ref,
    pool_ref, live_ref, code_ref, spread_ref, turn_ref, send, recv
):
    box, core = lax.axis_index("box"), lax.axis_index("help")
    z_at, other = box // PLANE, 1 - core
    above, below = (box + 1) % BOXES, (box + BOXES - 1) % BOXES
    near = ((above, 0, 0), (above, 1, 0), (below, 0, 2), (below, 1, 2), (box, other, 1))
    line = [((z_at + step) % Z_SIZE * PLANE + box % PLANE, core) for step in range(1, Z_SIZE)]
    barrier = pltpu.get_barrier_semaphore()
    for to_box, to_core, _ in near:
        pl.semaphore_signal(barrier, inc=1, device_id=(to_box, to_core), device_id_type=MESH)
    for target in line:
        pl.semaphore_signal(barrier, inc=1, device_id=target, device_id_type=MESH)

    lane = lax.broadcasted_iota(jnp.int32, (1, BS), 1)
    mine = 2 + core
    live = jnp.zeros((1, BS), jnp.int32)
    for block in range(BLK_DEV):
        count = counts_ref[block]
        live = jnp.where(lane == block, count, live)
        for axis in range(3):
            pool_ref[mine, block, axis : axis + 1, :] = pos_ref[axis, block : block + 1, :]
        pool_ref[mine, block, 3:4, :] = jnp.where(lane < count, weight_ref[block : block + 1, :], 0.0)
        pool_ref[mine, block, 4:8, :] = jnp.zeros((4, BS), jnp.float32)
    live_ref[mine] = live
    row = lax.broadcasted_iota(jnp.int32, (PRIM_DEV, BS), 0)
    col = lax.broadcasted_iota(jnp.int32, (PRIM_DEV, BS), 1)
    over = jnp.concatenate([region_ref[...], jnp.zeros((1, BS - PRIM_DEV), jnp.int32)], axis=1)
    down = jnp.sum(jnp.where(row == col, over, 0), axis=1, keepdims=True)
    rank = jnp.sum(jnp.where((down == over) & (row < col), 1, 0), axis=0, keepdims=True)
    code_ref[z_at] = jnp.where(lane < PRIM_DEV, 2 * over + rank, -1)

    pl.semaphore_wait(barrier, 12)

    def block_copy(slot, kind, target):
        ref = (pool_ref, live_ref)[kind]
        return pltpu.make_async_remote_copy(
            src_ref=ref.at[mine],
            dst_ref=ref.at[slot],
            send_sem=send.at[slot, kind],
            recv_sem=recv.at[slot, kind],
            device_id=target,
            device_id_type=MESH,
        )

    def code_copy(z_from, step):
        return pltpu.make_async_remote_copy(
            src_ref=code_ref.at[z_from],
            dst_ref=code_ref.at[z_from],
            send_sem=send.at[5 + step, 0],
            recv_sem=recv.at[6 + z_from, 0],
            device_id=line[step - 1],
            device_id_type=MESH,
        )

    sends = []
    for at, (to_box, to_core, move) in enumerate(near):
        for kind in range(2):
            ref = (pool_ref, live_ref)[kind]
            sends.append(
                pltpu.make_async_remote_copy(
                    src_ref=ref.at[mine],
                    dst_ref=ref.at[2 * move + core],
                    send_sem=send.at[at, kind],
                    recv_sem=recv.at[2 * move + core, kind],
                    device_id=(to_box, to_core),
                    device_id_type=MESH,
                )
            )
    for step in range(1, Z_SIZE):
        sends.append(code_copy(z_at, step))
    for copy in sends:
        copy.start()
    row = lax.broadcasted_iota(jnp.int32, (128, 128), 0)
    col = lax.broadcasted_iota(jnp.int32, (128, 128), 1)
    for part in range(8):
        hit = col - part * NBIN == row // 8
        spread_ref[part] = jnp.where(hit, 1.0, 0.0).astype(jnp.bfloat16)
    turn_ref[...] = turn_matrix()
    for slot in (0, 1, 4, 5, 2 + other):
        for kind in range(2):
            block_copy(slot, kind, (box, other)).wait_recv()
    for step in range(1, Z_SIZE):
        code_copy((z_at + step) % Z_SIZE, step).wait_recv()
    for copy in sends:
        copy.wait_send()


def near(counts, pos, weight, regions):
    return pl.pallas_call(
        near_kernel,
        out_shape=(
            jax.ShapeDtypeStruct((6, BLK_DEV, 8, BS), jnp.float32),
            jax.ShapeDtypeStruct((6, 1, BS), jnp.int32),
            jax.ShapeDtypeStruct((Z_SIZE, 1, BS), jnp.int32),
            jax.ShapeDtypeStruct((8, 128, 128), jnp.bfloat16),
            jax.ShapeDtypeStruct((256, 256), jnp.bfloat16),
        ),
        in_specs=[pl.BlockSpec(memory_space=pltpu.SMEM)]
        + [pl.BlockSpec(memory_space=pltpu.VMEM)] * 3,
        out_specs=(pl.BlockSpec(memory_space=pltpu.VMEM),) * 5,
        scratch_shapes=[pltpu.SemaphoreType.DMA((13, 2)), pltpu.SemaphoreType.DMA((14, 2))],
        compiler_params=pltpu.CompilerParams(
            collective_id=0, has_side_effects=True, vmem_limit_bytes=8 << 20
        ),
        name="near",
    )(counts, pos, weight, regions)


def pair_kernel(
    list_ref, pool_ref, live_ref, code_ref, pos_ref, weight_ref, spread, turn_ref,
    coef_ref, rows_ref, table_ref, packed, basis, spline, acc, diag, live, sem
):
    tile = pl.program_id(0)
    box, core = lax.axis_index("box"), lax.axis_index("help")
    lane = lax.broadcasted_iota(jnp.int32, (8, BS), 1)

    @pl.when(tile == 0)
    def _():
        fetch = pltpu.make_async_copy(live_ref, live, sem)
        fetch.start()
        turn = lax.broadcasted_iota(jnp.int32, (2 * PEERS, BS), 0)
        over = lax.broadcasted_iota(jnp.int32, (2 * PEERS, BS), 1)
        x_to, y_to = (box // 4 + turn // 16) % 4, (box + turn // 4) % 4
        owner = (box // PLANE * PLANE + x_to * 4 + y_to) * 2 + (core + turn // 2) % 2
        wanted = owner * 2 + turn % 2
        table = jnp.zeros((2 * PEERS, BS), jnp.int32)
        for z_from in range(Z_SIZE):
            found = jnp.max(
                jnp.where(code_ref[z_from] == wanted, over, -1), axis=1, keepdims=True
            )
            table = jnp.where(over == z_from, found, table)
        table_ref[...] = table
        fetch.wait()

    packed[...] = jnp.zeros_like(packed)
    filled = jnp.int32(0)
    for slot in range(LIST):
        listed = list_ref[tile, slot]
        used = listed >= 0
        listed = jnp.maximum(listed, 0)
        owner, inner = listed >> 3, listed & (BLK_DEV - 1)
        place = jnp.where(used, (((owner >> 1) - box + 1) & (BOXES - 1)) * 2 + (owner & 1), 0)
        block = pool_ref[place, inner]
        base = filled >> 7
        shift = filled & (BS - 1)
        moved = pltpu.roll(block, shift, 1)
        low = jnp.where((lane >= shift) & used, moved, packed[base])
        packed[base] = low
        high = jnp.where((lane < shift) & used, moved, packed[base + 1])
        packed[base + 1] = high
        filled = filled + jnp.where(used, live[place, 0, inner], 0)
    chunks = (filled + 2 * BS - 1) >> 8

    acc[...] = jnp.zeros_like(acc)
    own = lax.broadcasted_iota(jnp.int32, (PT, PRIM_DEV), 0) + tile * PT
    own = own == lax.broadcasted_iota(jnp.int32, (PT, PRIM_DEV), 1)

    def column(values):
        return jnp.sum(jnp.where(own, values, 0.0), axis=1, keepdims=True)

    px, py, pz = [column(pos_ref[axis : axis + 1, :]) for axis in range(3)]
    scale_column = column(weight_ref[...]) * (1.0 / math.sqrt(LIST * BS))
    bin_step = 1.0 / (NBIN + 1)

    def chunk_step(chunk, carry):
        geometry = []
        for half in range(2):
            rows = packed[2 * chunk + half]
            dx = rows[0:1, :] - px
            dy = rows[1:2, :] - py
            dz = rows[2:3, :] - pz
            weight = jnp.broadcast_to(rows[3:4, :], (PT, BS))
            radius = jnp.sqrt(dx * dx + dy * dy + dz * dz)
            inverse = 1.0 / jnp.maximum(radius, 0.5 * bin_step)
            geometry.append((dx * inverse, dy * inverse, dz * inverse))
            place = radius * float(NBIN + 1)
            whole = jnp.floor(place)
            part = place - whole
            upper = weight * part
            lower = weight * (1.0 - part)
            cols = slice(half * BS, (half + 1) * BS)
            above = jnp.where(whole == 0.0, upper, 0.0)
            hats = []
            for bin_at in range(NBIN):
                here = whole == float(bin_at + 1)
                hats.append(jnp.where(here, lower, above))
                above = jnp.where(here, upper, 0.0)
            for side in range(2):
                part_rows = slice(side * 8, side * 8 + 8)
                for bin_at in range(0, NBIN, 2):
                    both = jnp.concatenate([hats[bin_at][part_rows], hats[bin_at + 1][part_rows]])
                    at = side * 128 + bin_at * 8
                    spline[at : at + 16, cols] = both.astype(jnp.bfloat16)
        angular = [[None, None], [None, None]]
        for orders in GROUPS:
            for half in range(2):
                ux, uy, uz = geometry[half]
                cols = slice(half * BS, (half + 1) * BS)
                for m_order in orders:
                    if m_order == 1:
                        angular[half] = [ux, uy]
                    elif m_order > 1:
                        cos_part, sin_part = angular[half]
                        angular[half] = [
                            cos_part * ux - sin_part * uy,
                            sin_part * ux + cos_part * uy,
                        ]
                    older, newer = None, None
                    start = first_row(m_order)
                    count = LMAX + 1 - m_order
                    for degree in range(m_order, LMAX + 1):
                        if degree == m_order:
                            current = None
                        elif degree == m_order + 1:
                            current = uz
                        else:
                            ratio = (degree + m_order - 1) * (degree - m_order - 1) / (
                                (2 * degree - 1) * (2 * degree - 3)
                            )
                            if older is None:
                                current = uz * newer - ratio
                            else:
                                current = uz * newer - ratio * older
                        older, newer = newer, current
                        scale = harmonic_scale(m_order, degree)
                        at = (start + degree - m_order) * PT
                        if current is None:
                            scaled = None
                        else:
                            scaled = current * scale
                        if m_order == 0:
                            value = jnp.full((PT, BS), scale, jnp.float32) if scaled is None else scaled
                            basis[at : at + PT, cols] = value.astype(jnp.bfloat16)
                        else:
                            for kind in range(2):
                                turn = angular[half][kind]
                                value = turn * scale if scaled is None else scaled * turn
                                low = at + kind * count * PT
                                basis[low : low + PT, cols] = value.astype(jnp.bfloat16)
            first = first_row(orders[0]) * PT
            last = NHARM * PT if orders[-1] == LMAX else first_row(orders[-1] + 1) * PT
            product = lax.dot_general(
                basis[first:last, :],
                spline[...],
                (((1,), (1,)), ((), ())),
                preferred_element_type=jnp.float32,
            ).reshape(-1, 2, 8, 2 * BS)
            wanted = jnp.concatenate(
                [product[:, 0:1, :, 0:128], product[:, 1:2, :, 128:256]], axis=1
            )
            acc[first:last, :] += wanted.reshape(last - first, 128)
        return carry

    lax.fori_loop(0, chunks, chunk_step, 0)

    row = lax.broadcasted_iota(jnp.int32, (PT, 128), 0)
    col = lax.broadcasted_iota(jnp.int32, (PT, 128), 1)
    keep = jnp.where((col & 7) == (row & 7), scale_column, 0.0)
    for harm in range(128):
        if harm < NHARM:
            value = (acc[harm * PT : (harm + 1) * PT, :] * keep).astype(jnp.bfloat16)
        else:
            value = jnp.zeros((PT, 128), jnp.bfloat16)
        diag[harm % 8, (harm // 8) * PT : (harm // 8 + 1) * PT, :] = value
    total = jnp.zeros((256, 128), jnp.float32)
    for part in range(8):
        total = total + jnp.dot(diag[part], spread[part], preferred_element_type=jnp.float32)
    rows = total.astype(jnp.bfloat16)
    for group in range(15):
        coef_ref[:, group * 128 : (group + 1) * 128] = rows[group * PT : (group + 1) * PT, :]
    coef_ref[:, 1920:FEAT] = rows[15 * PT : 16 * PT, : FEAT - 1920]
    turned = jnp.dot(turn_ref[...], rows, preferred_element_type=jnp.float32)
    rows_ref[...] = turned.astype(jnp.bfloat16).reshape(PT, 16, 128)


def pair_sums(lists, *operands):
    tiles = lists.shape[0]
    live = operands[1]
    return pl.pallas_call(
        pair_kernel,
        out_shape=(
            jax.ShapeDtypeStruct((tiles * PT, FEAT), jnp.bfloat16),
            jax.ShapeDtypeStruct((tiles * PT, 16, 128), jnp.bfloat16),
            jax.ShapeDtypeStruct((2 * PEERS, BS), jnp.int32),
        ),
        grid_spec=pltpu.PrefetchScalarGridSpec(
            num_scalar_prefetch=1,
            grid=(tiles,),
            in_specs=[pl.BlockSpec(memory_space=pltpu.VMEM)] * len(operands),
            out_specs=(
                pl.BlockSpec((PT, FEAT), lambda t, *_: (t, 0)),
                pl.BlockSpec((PT, 16, 128), lambda t, *_: (t, 0, 0)),
                pl.BlockSpec((2 * PEERS, BS), lambda t, *_: (0, 0)),
            ),
            scratch_shapes=[
                pltpu.VMEM((2 * ((LIST + 1) // 2) + 2, 8, BS), jnp.float32),
                pltpu.VMEM((NHARM * PT, 2 * BS), jnp.bfloat16),
                pltpu.VMEM((NBIN * PT, 2 * BS), jnp.bfloat16),
                pltpu.VMEM((NHARM * PT, 128), jnp.float32),
                pltpu.VMEM((8, 256, 128), jnp.bfloat16),
                pltpu.SMEM(live.shape, live.dtype),
                pltpu.SemaphoreType.DMA(()),
            ],
        ),
        compiler_params=pltpu.CompilerParams(vmem_limit_bytes=40 << 20),
        name="pair_sums",
    )(lists, *operands)


def gram_tiles():
    tiles = []
    for m_order, (cos_start, sin_start, length) in enumerate(order_slices(LMAX, NBIN)):
        for kind, start in enumerate((cos_start, sin_start)):
            if start >= 0:
                for part in range(-(-length // 128)):
                    width = min(128, length - 128 * part)
                    tiles.append((m_order, kind, start + 128 * part, width))
    return tiles


def gram_flatten(gram, out_ref, base, count):
    lane = lax.broadcasted_iota(jnp.int32, (2 * count, 128), 1)
    for rest in range(8):
        for part in range(-(-count // 8)):
            units = min(8, count - 8 * part)
            shift = rest * count % 8
            at = base + rest * count // 8 + part
            value = gram[part, pl.ds(rest, 2 * count, stride=8), :] * (1.0 / PRIM_DEV)
            if shift:
                value = pltpu.roll(value, 16 * shift, 1)
            window = pl.ds(at, 2 * count, stride=count)
            keep = (lane >= 16 * shift) & (lane < 16 * (shift + units))
            out_ref[window, :] = jnp.where(keep, value, out_ref[window, :])
            if shift + units > 8:
                window = pl.ds(at + 1, 2 * count, stride=count)
                keep = lane < 16 * (shift + units - 8)
                out_ref[window, :] = jnp.where(keep, value, out_ref[window, :])


PLANE_MOVES = (
    (1, 0), (3, 0), (0, 1), (0, 3), (1, 1), (3, 3), (1, 3), (3, 1),
    (2, 0), (0, 2), (2, 2), (2, 1), (1, 2), (2, 3), (3, 2),
)
BATCHES = ((0, 1), (1, 2), (3, 2), (5, 2), (7, 1))


def regions_kernel(table_ref, rows_ref, out_ref, *scratch):
    held = (rows_ref,) + scratch[:7]
    stage, come, feats, shifts, plain, flipped, gram = scratch[7:14]
    ring_send, ring_recv, plane_send, plane_recv = scratch[14:]
    box, core = lax.axis_index("box"), lax.axis_index("help")
    z_at, x_at, y_at = box // PLANE, (box // 4) % 4, box % 4
    ring = (
        ((z_at + 1) % Z_SIZE * PLANE + box % PLANE, core),
        ((z_at + Z_SIZE - 1) % Z_SIZE * PLANE + box % PLANE, core),
    )

    def peer(turn):
        x_to, y_to = (x_at + turn // 8) % 4, (y_at + turn // 2 % 4) % 4
        return (z_at * PLANE + x_to * 4 + y_to, (core + turn % 2) % 2)

    barrier = pltpu.get_barrier_semaphore()
    for way in range(2):
        pl.semaphore_signal(barrier, inc=1, device_id=ring[way], device_id_type=MESH)

    def greet(turn, carry):
        pl.semaphore_signal(barrier, inc=1, device_id=peer(turn), device_id_type=MESH)
        return carry

    lax.fori_loop(1, PEERS, greet, 0)
    pl.semaphore_wait(barrier, PEERS + 1)

    def ring_copy(way, step, half):
        from_at = 0 if step == 1 else 2 * (step - 1) - 1 + way
        to_at = 7 if step == 4 else 2 * step - 1 + way
        part = pl.ds(half * (PRIM_DEV // 2), PRIM_DEV // 2)
        return pltpu.make_async_remote_copy(
            src_ref=held[from_at].at[part],
            dst_ref=held[to_at].at[part],
            send_sem=ring_send.at[way, step - 1, half],
            recv_sem=ring_recv.at[way, step - 1, half],
            device_id=ring[way],
            device_id_type=MESH,
        )

    def deal(batch):
        first, number = BATCHES[batch]

        def fill(turn, target):
            for source in range(first, first + number):
                z_from = (z_at + SOURCE_MOVES[source] + Z_SIZE) % Z_SIZE
                for slot in range(2):
                    row = table_ref[turn * 2 + slot, z_from]
                    value = held[source][jnp.maximum(row, 0)]
                    target[turn, source, slot] = jnp.where(row >= 0, value, jnp.zeros_like(value))

        def one_peer(turn):
            fill(turn, stage)
            pltpu.make_async_remote_copy(
                src_ref=stage.at[turn, pl.ds(first, number)],
                dst_ref=come.at[turn, pl.ds(first, number)],
                send_sem=plane_send.at[batch],
                recv_sem=plane_recv.at[batch],
                device_id=peer(turn),
                device_id_type=MESH,
            ).start()

        def one_core(core_move, carry):
            for x_move, y_move in PLANE_MOVES:
                one_peer(x_move * 8 + y_move * 2 + core_move)
            return carry

        lax.fori_loop(0, 2, one_core, 0)
        one_peer(1)
        fill(0, come)

    tiles = gram_tiles()
    across = (((1,), (1,)), ((), ()))

    def prepare():
        row = lax.broadcasted_iota(jnp.int32, (128, 128), 0)
        col = lax.broadcasted_iota(jnp.int32, (128, 128), 1)
        for unit in range(-7, 8):
            hit = row == col + 16 * unit
            shifts[unit + 7] = jnp.where(hit, 1.0, 0.0).astype(jnp.bfloat16)

    def collect(batch):
        first, number = BATCHES[batch]
        arrived = come.at[pl.ds(1, PEERS - 1), pl.ds(first, number)]
        pltpu.make_async_copy(arrived, arrived, plane_recv.at[batch]).wait()
        turn = turn_matrix()
        for source in range(number):

            def regroup(step, carry, source=source):
                block = come[pl.ds(step * 8, 8), first + source].reshape(256, 128)
                moved = jnp.dot(turn, block, preferred_element_type=jnp.float32)
                at = pl.multiple_of(source * 64 + step * 16, 16)
                feats[:, pl.ds(at, 16), :] = moved.astype(jnp.bfloat16).reshape(16, 16, 128)
                return carry

            lax.fori_loop(0, 4, regroup, 0, unroll=True)
        size = 64 * number
        at = (384, 0, 128, 256, 448)[batch]
        for tile, (_, _, start, width) in enumerate(tiles):
            group, skip = start // 128, start % 128 // 16
            here = feats[group, 0:size, :]
            over = lax.dot_general(
                shifts[7 - skip], here, across, preferred_element_type=jnp.float32
            )
            if skip == 0:
                down = here
            else:
                down = jnp.dot(here, shifts[7 + skip], preferred_element_type=jnp.float32)
                if skip * 16 + width > 128:
                    there = feats[group + 1, 0:size, :]
                    down += jnp.dot(there, shifts[skip - 1], preferred_element_type=jnp.float32)
                    over += lax.dot_general(
                        shifts[15 - skip], there, across, preferred_element_type=jnp.float32
                    )
            plain[tile, at : at + size, :] = down.astype(jnp.bfloat16)
            flipped[tile, :, at : at + size] = over.astype(jnp.bfloat16)

    for half in range(2):
        for way in range(2):
            ring_copy(way, 1, half).start()
    deal(0)
    prepare()
    for step in range(1, 4):
        for half in range(2):
            for way in range(2):
                ring_copy(way, step, half).wait_recv()
                if step < 3 or half == way:
                    ring_copy(way, step + 1, half).start()
            if half == 0 and step > 1:
                collect(step - 2)
        deal(step)
    for way in range(2):
        ring_copy(way, 4, way).wait_recv()
    deal(4)
    for batch in range(2, 5):
        collect(batch)

    base = 0
    for m_order, (_, _, length) in enumerate(order_slices(LMAX, NBIN)):
        parts = -(-length // 128)
        for kind in range(2):
            mine = [at for at, tile in enumerate(tiles) if tile[:2] == (m_order, kind)]
            for up, up_tile in enumerate(mine):
                for over, over_tile in enumerate(mine):
                    product = jnp.dot(
                        flipped[up_tile], plain[over_tile], preferred_element_type=jnp.float32
                    )
                    at = (over, slice(up * 128, up * 128 + 128))
                    if kind == 0:
                        gram[at] = product
                    else:
                        gram[at] += product
        gram_flatten(gram, out_ref, base, length // NBIN)
        base += length * length // 128

    for step in range(1, 5):
        for half in range(2):
            for way in range(2):
                if step < 4 or half == way:
                    ring_copy(way, step, half).wait_send()
    for batch, (first, number) in enumerate(BATCHES):
        sent = stage.at[pl.ds(1, PEERS - 1), pl.ds(first, number)]
        pltpu.make_async_copy(sent, sent, plane_send.at[batch]).wait()


def region_products(table, rows):
    shape = (PEERS, Z_SIZE, 2, 16, 128)
    total = sum(length * length for _, _, length in order_slices(LMAX, NBIN))
    tiles = len(gram_tiles())
    row_total = PEERS * Z_SIZE * 2
    return pl.pallas_call(
        regions_kernel,
        out_shape=jax.ShapeDtypeStruct((total // 128, 128), jnp.float32),
        in_specs=[
            pl.BlockSpec(memory_space=pltpu.SMEM),
            pl.BlockSpec(memory_space=pltpu.VMEM),
        ],
        out_specs=pl.BlockSpec(memory_space=pltpu.VMEM),
        scratch_shapes=[pltpu.VMEM(rows.shape, rows.dtype)] * 7
        + [
            pltpu.VMEM(shape, rows.dtype),
            pltpu.VMEM(shape, rows.dtype),
            pltpu.VMEM((16, 128, 128), rows.dtype),
            pltpu.VMEM((15, 128, 128), rows.dtype),
            pltpu.VMEM((tiles, row_total, 128), rows.dtype),
            pltpu.VMEM((tiles, 128, row_total), rows.dtype),
            pltpu.VMEM((2, 256, 128), jnp.float32),
            pltpu.SemaphoreType.DMA((2, 4, 2)),
            pltpu.SemaphoreType.DMA((2, 4, 2)),
            pltpu.SemaphoreType.DMA((5,)),
            pltpu.SemaphoreType.DMA((5,)),
        ],
        compiler_params=pltpu.CompilerParams(
            collective_id=1, has_side_effects=True, vmem_limit_bytes=40 << 20
        ),
        name="region_products",
    )(table, rows)


def shards(prim_pos, prim_weight, sec_pos, sec_weight, sec_counts, tile_lists, region_of):
    pool, live, codes, spread, turn = near(
        sec_counts, sec_pos.transpose(1, 0, 2), sec_weight, region_of.reshape(1, -1)
    )
    coefficients, rows, table = pair_sums(
        tile_lists, pool, live, codes, prim_pos, prim_weight.reshape(1, -1), spread, turn
    )
    region_tensor = region_products(table, rows).reshape(1, -1)
    return (coefficients, region_tensor)


def solution(mesh):
    placed = (
        P(None, ("box", "help")),
        P(("box", "help")),
        P(("box", "help"), None, None),
        P(("box", "help"), None),
        P(("box", "help")),
        P(("box", "help"), None),
        P(("box", "help"), None),
    )
    return jax.shard_map(
        shards,
        mesh=mesh,
        in_specs=placed,
        out_specs=(P(("box", "help"), None), P(("box", "help"), None)),
        check_vma=False,
    )
```

```python
import functools
import math

import jax
import jax.numpy as jnp
from jax import lax
from jax.experimental import pallas as pl
from jax.experimental.pallas import tpu as pltpu
from jax.sharding import PartitionSpec as P

LMAX = 10
NBIN = 16
BS = 128
LIST = 12
PT = 16
PRIM_DEV = 64
NHARM = (LMAX + 1) ** 2
FEAT = NHARM * NBIN
BOXES = 128
BLK_DEV = 8
Z_SIZE = 8
PLANE = 16
SOURCE_MOVES = (0, -1, 1, -2, 2, -3, 3, 4)
PEERS = 2 * PLANE
MESH = pl.DeviceIdType.MESH

GROUPS = ((0, 1, 2, 3, 4, 5, 6, 7, 8, 9, 10),)


def order_slices(degree_top, bin_count):
    slices = []
    position = 0
    for m_order in range(degree_top + 1):
        length = (degree_top + 1 - m_order) * bin_count
        if m_order == 0:
            slices.append((position, -1, length))
            position = position + length
        else:
            slices.append((position, position + length, length))
            position = position + 2 * length
    return slices


def harmonic_scale(m_order, degree):
    factor = math.sqrt(
        (2 * degree + 1)
        / (4.0 * math.pi)
        * math.factorial(degree - m_order)
        / math.factorial(degree + m_order)
    )
    if m_order > 0:
        factor = factor * math.sqrt(2.0)
    lead = 1.0
    for odd_value in range(1, 2 * m_order, 2):
        lead = lead * odd_value
    for step in range(m_order + 1, degree + 1):
        lead = lead * (2 * step - 1) / (step - m_order)
    return factor * lead


def first_row(m_order):
    return order_slices(LMAX, 1)[m_order][0]


def turn_matrix():
    row = lax.broadcasted_iota(jnp.int32, (256, 256), 0)
    col = lax.broadcasted_iota(jnp.int32, (256, 256), 1)
    return jnp.where(col == (row % 16) * 16 + row // 16, 1.0, 0.0).astype(jnp.bfloat16)


def near_kernel(
    counts_ref, pos_ref, weight_ref, region_ref,
    pool_ref, live_ref, code_ref, spread_ref, turn_ref, send, recv
):
    box, core = lax.axis_index("box"), lax.axis_index("help")
    z_at, other = box // PLANE, 1 - core
    above, below = (box + 1) % BOXES, (box + BOXES - 1) % BOXES
    near = ((above, 0, 0), (above, 1, 0), (below, 0, 2), (below, 1, 2), (box, other, 1))
    line = [((z_at + step) % Z_SIZE * PLANE + box % PLANE, core) for step in range(1, Z_SIZE)]
    barrier = pltpu.get_barrier_semaphore()
    for to_box, to_core, _ in near:
        pl.semaphore_signal(barrier, inc=1, device_id=(to_box, to_core), device_id_type=MESH)
    for target in line:
        pl.semaphore_signal(barrier, inc=1, device_id=target, device_id_type=MESH)

    lane = lax.broadcasted_iota(jnp.int32, (1, BS), 1)
    mine = 2 + core
    live = jnp.zeros((1, BS), jnp.int32)
    for block in range(BLK_DEV):
        count = counts_ref[block]
        live = jnp.where(lane == block, count, live)
        for axis in range(3):
            pool_ref[mine, block, axis : axis + 1, :] = pos_ref[axis, block : block + 1, :]
        pool_ref[mine, block, 3:4, :] = jnp.where(lane < count, weight_ref[block : block + 1, :], 0.0)
    live_ref[mine] = live
    row = lax.broadcasted_iota(jnp.int32, (PRIM_DEV, BS), 0)
    col = lax.broadcasted_iota(jnp.int32, (PRIM_DEV, BS), 1)
    over = jnp.concatenate([region_ref[...], jnp.zeros((1, BS - PRIM_DEV), jnp.int32)], axis=1)
    down = jnp.sum(jnp.where(row == col, over, 0), axis=1, keepdims=True)
    rank = jnp.sum(jnp.where((down == over) & (row < col), 1, 0), axis=0, keepdims=True)
    code_ref[z_at] = jnp.where(lane < PRIM_DEV, 2 * over + rank, -1)

    pl.semaphore_wait(barrier, 12)

    def push(kind, ref, from_at, to_at, target):
        pltpu.make_async_remote_copy(
            src_ref=ref.at[from_at],
            dst_ref=ref.at[to_at],
            send_sem=send.at[kind],
            recv_sem=recv.at[kind],
            device_id=target,
            device_id_type=MESH,
        ).start()

    for step in (4, 3, 5, 2, 6, 1, 7):
        push(2, code_ref, z_at, z_at, line[step - 1])
    for to_box, to_core, move in near:
        push(0, pool_ref, mine, 2 * move + core, (to_box, to_core))
        push(1, live_ref, mine, 2 * move + core, (to_box, to_core))
    row = lax.broadcasted_iota(jnp.int32, (128, 128), 0)
    col = lax.broadcasted_iota(jnp.int32, (128, 128), 1)
    for part in range(8):
        hit = col - part * NBIN == row // 8
        spread_ref[part] = jnp.where(hit, 1.0, 0.0).astype(jnp.bfloat16)
    turn_ref[...] = turn_matrix()
    for sems in (recv, send):
        for kind, (ref, number) in enumerate(((pool_ref, 5), (live_ref, 5), (code_ref, 7))):
            moved = ref.at[pl.ds(0, number)]
            pltpu.make_async_copy(moved, moved, sems.at[kind]).wait()


def near(counts, pos, weight, regions):
    return pl.pallas_call(
        near_kernel,
        out_shape=(
            jax.ShapeDtypeStruct((6, BLK_DEV, 4, BS), jnp.float32),
            jax.ShapeDtypeStruct((6, 1, BS), jnp.int32),
            jax.ShapeDtypeStruct((Z_SIZE, 1, BS), jnp.int32),
            jax.ShapeDtypeStruct((8, 128, 128), jnp.bfloat16),
            jax.ShapeDtypeStruct((256, 256), jnp.bfloat16),
        ),
        in_specs=[pl.BlockSpec(memory_space=pltpu.SMEM)]
        + [pl.BlockSpec(memory_space=pltpu.VMEM)] * 3,
        out_specs=(pl.BlockSpec(memory_space=pltpu.VMEM),) * 5,
        scratch_shapes=[pltpu.SemaphoreType.DMA((3,)), pltpu.SemaphoreType.DMA((3,))],
        compiler_params=pltpu.CompilerParams(
            collective_id=0, has_side_effects=True, vmem_limit_bytes=8 << 20
        ),
        name="near",
    )(counts, pos, weight, regions)


def pair_kernel(
    list_ref, pool_ref, live_ref, code_ref, pos_ref, weight_ref, spread, turn_ref,
    coef_ref, rows_ref, table_ref, packed, basis, spline, acc, diag, live, sem
):
    tile = pl.program_id(0)
    box, core = lax.axis_index("box"), lax.axis_index("help")
    lane = lax.broadcasted_iota(jnp.int32, (4, BS), 1)

    @pl.when(tile == 0)
    def _():
        fetch = pltpu.make_async_copy(live_ref, live, sem)
        fetch.start()
        turn = lax.broadcasted_iota(jnp.int32, (2 * PEERS, BS), 0)
        over = lax.broadcasted_iota(jnp.int32, (2 * PEERS, BS), 1)
        x_to, y_to = (box // 4 + turn // 16) % 4, (box + turn // 4) % 4
        owner = (box // PLANE * PLANE + x_to * 4 + y_to) * 2 + (core + turn // 2) % 2
        wanted = owner * 2 + turn % 2
        table = jnp.zeros((2 * PEERS, BS), jnp.int32)
        for z_from in range(Z_SIZE):
            found = jnp.max(
                jnp.where(code_ref[z_from] == wanted, over, -1), axis=1, keepdims=True
            )
            table = jnp.where(over == z_from, found, table)
        table_ref[...] = table
        fetch.wait()

    packed[...] = jnp.zeros_like(packed)
    filled = jnp.int32(0)
    for slot in range(LIST):
        listed = list_ref[tile, slot]
        used = listed >= 0
        listed = jnp.maximum(listed, 0)
        owner, inner = listed >> 3, listed & (BLK_DEV - 1)
        place = jnp.where(used, (((owner >> 1) - box + 1) & (BOXES - 1)) * 2 + (owner & 1), 0)
        block = pool_ref[place, inner]
        base = filled >> 7
        shift = filled & (BS - 1)
        moved = pltpu.roll(block, shift, 1)
        low = jnp.where((lane >= shift) & used, moved, packed[base])
        packed[base] = low
        high = jnp.where((lane < shift) & used, moved, packed[base + 1])
        packed[base + 1] = high
        filled = filled + jnp.where(used, live[place, 0, inner], 0)
    chunks = (filled + 2 * BS - 1) >> 8

    acc[...] = jnp.zeros_like(acc)
    own = lax.broadcasted_iota(jnp.int32, (PT, PRIM_DEV), 0) + tile * PT
    own = own == lax.broadcasted_iota(jnp.int32, (PT, PRIM_DEV), 1)

    def column(values):
        return jnp.sum(jnp.where(own, values, 0.0), axis=1, keepdims=True)

    px, py, pz = [column(pos_ref[axis : axis + 1, :]) for axis in range(3)]
    scale_column = column(weight_ref[...]) * (1.0 / math.sqrt(LIST * BS))
    bin_step = 1.0 / (NBIN + 1)

    def chunk_step(chunk, carry):
        geometry = []
        for half in range(2):
            rows = packed[2 * chunk + half]
            dx = rows[0:1, :] - px
            dy = rows[1:2, :] - py
            dz = rows[2:3, :] - pz
            weight = jnp.broadcast_to(rows[3:4, :], (PT, BS))
            radius = jnp.sqrt(dx * dx + dy * dy + dz * dz)
            inverse = 1.0 / jnp.maximum(radius, 0.5 * bin_step)
            geometry.append((dx * inverse, dy * inverse, dz * inverse))
            place = radius * float(NBIN + 1)
            whole = jnp.floor(place)
            part = place - whole
            upper = weight * part
            lower = weight * (1.0 - part)
            cols = slice(half * BS, (half + 1) * BS)
            above = jnp.where(whole == 0.0, upper, 0.0)
            hats = []
            for bin_at in range(NBIN):
                here = whole == float(bin_at + 1)
                hats.append(jnp.where(here, lower, above))
                above = jnp.where(here, upper, 0.0)
            for side in range(2):
                part_rows = slice(side * 8, side * 8 + 8)
                for bin_at in range(0, NBIN, 2):
                    both = jnp.concatenate([hats[bin_at][part_rows], hats[bin_at + 1][part_rows]])
                    at = side * 128 + bin_at * 8
                    spline[at : at + 16, cols] = both.astype(jnp.bfloat16)
        angular = [[None, None], [None, None]]
        for orders in GROUPS:
            for half in range(2):
                ux, uy, uz = geometry[half]
                cols = slice(half * BS, (half + 1) * BS)
                for m_order in orders:
                    if m_order == 1:
                        angular[half] = [ux, uy]
                    elif m_order > 1:
                        cos_part, sin_part = angular[half]
                        angular[half] = [
                            cos_part * ux - sin_part * uy,
                            sin_part * ux + cos_part * uy,
                        ]
                    older, newer = None, None
                    start = first_row(m_order)
                    count = LMAX + 1 - m_order
                    for degree in range(m_order, LMAX + 1):
                        if degree == m_order:
                            current = None
                        elif degree == m_order + 1:
                            current = uz
                        else:
                            ratio = (degree + m_order - 1) * (degree - m_order - 1) / (
                                (2 * degree - 1) * (2 * degree - 3)
                            )
                            if older is None:
                                current = uz * newer - ratio
                            else:
                                current = uz * newer - ratio * older
                        older, newer = newer, current
                        scale = harmonic_scale(m_order, degree)
                        at = (start + degree - m_order) * PT
                        if current is None:
                            scaled = None
                        else:
                            scaled = current * scale
                        if m_order == 0:
                            value = jnp.full((PT, BS), scale, jnp.float32) if scaled is None else scaled
                            basis[at : at + PT, cols] = value.astype(jnp.bfloat16)
                        else:
                            for kind in range(2):
                                turn = angular[half][kind]
                                value = turn * scale if scaled is None else scaled * turn
                                low = at + kind * count * PT
                                basis[low : low + PT, cols] = value.astype(jnp.bfloat16)
            first = first_row(orders[0]) * PT
            last = NHARM * PT if orders[-1] == LMAX else first_row(orders[-1] + 1) * PT
            product = lax.dot_general(
                basis[first:last, :],
                spline[...],
                (((1,), (1,)), ((), ())),
                preferred_element_type=jnp.float32,
            ).reshape(-1, 2, 8, 2 * BS)
            wanted = jnp.concatenate(
                [product[:, 0:1, :, 0:128], product[:, 1:2, :, 128:256]], axis=1
            )
            acc[first:last, :] += wanted.reshape(last - first, 128)
        return carry

    lax.fori_loop(0, chunks, chunk_step, 0)

    row = lax.broadcasted_iota(jnp.int32, (PT, 128), 0)
    col = lax.broadcasted_iota(jnp.int32, (PT, 128), 1)
    keep = jnp.where((col & 7) == (row & 7), scale_column, 0.0)
    for harm in range(128):
        if harm < NHARM:
            value = (acc[harm * PT : (harm + 1) * PT, :] * keep).astype(jnp.bfloat16)
        else:
            value = jnp.zeros((PT, 128), jnp.bfloat16)
        diag[harm % 8, (harm // 8) * PT : (harm // 8 + 1) * PT, :] = value
    total = jnp.zeros((256, 128), jnp.float32)
    for part in range(8):
        total = total + jnp.dot(diag[part], spread[part], preferred_element_type=jnp.float32)
    rows = total.astype(jnp.bfloat16)
    for group in range(15):
        coef_ref[:, group * 128 : (group + 1) * 128] = rows[group * PT : (group + 1) * PT, :]
    coef_ref[:, 1920:FEAT] = rows[15 * PT : 16 * PT, : FEAT - 1920]
    turned = jnp.dot(turn_ref[...], rows, preferred_element_type=jnp.float32)
    rows_ref[...] = turned.astype(jnp.bfloat16).reshape(PT, 16, 128)


def pair_sums(lists, *operands):
    tiles = lists.shape[0]
    live = operands[1]
    return pl.pallas_call(
        pair_kernel,
        out_shape=(
            jax.ShapeDtypeStruct((tiles * PT, FEAT), jnp.bfloat16),
            jax.ShapeDtypeStruct((tiles * PT, 16, 128), jnp.bfloat16),
            jax.ShapeDtypeStruct((2 * PEERS, BS), jnp.int32),
        ),
        grid_spec=pltpu.PrefetchScalarGridSpec(
            num_scalar_prefetch=1,
            grid=(tiles,),
            in_specs=[pl.BlockSpec(memory_space=pltpu.VMEM)] * len(operands),
            out_specs=(
                pl.BlockSpec((PT, FEAT), lambda t, *_: (t, 0)),
                pl.BlockSpec((PT, 16, 128), lambda t, *_: (t, 0, 0)),
                pl.BlockSpec((2 * PEERS, BS), lambda t, *_: (0, 0)),
            ),
            scratch_shapes=[
                pltpu.VMEM((2 * ((LIST + 1) // 2) + 2, 4, BS), jnp.float32),
                pltpu.VMEM((NHARM * PT, 2 * BS), jnp.bfloat16),
                pltpu.VMEM((NBIN * PT, 2 * BS), jnp.bfloat16),
                pltpu.VMEM((NHARM * PT, 128), jnp.float32),
                pltpu.VMEM((8, 256, 128), jnp.bfloat16),
                pltpu.SMEM(live.shape, live.dtype),
                pltpu.SemaphoreType.DMA(()),
            ],
        ),
        compiler_params=pltpu.CompilerParams(vmem_limit_bytes=40 << 20),
        name="pair_sums",
    )(lists, *operands)


def gram_tiles():
    tiles = []
    for m_order, (cos_start, sin_start, length) in enumerate(order_slices(LMAX, NBIN)):
        for kind, start in enumerate((cos_start, sin_start)):
            if start >= 0:
                for part in range(-(-length // 128)):
                    width = min(128, length - 128 * part)
                    tiles.append((m_order, kind, start + 128 * part, width))
    return tiles


def gram_flatten(gram, out_ref, base, count):
    lane = lax.broadcasted_iota(jnp.int32, (2 * count, 128), 1)
    for rest in range(8):
        for part in range(-(-count // 8)):
            units = min(8, count - 8 * part)
            shift = rest * count % 8
            at = base + rest * count // 8 + part
            value = gram[part, pl.ds(rest, 2 * count, stride=8), :] * (1.0 / PRIM_DEV)
            if shift:
                value = pltpu.roll(value, 16 * shift, 1)
            window = pl.ds(at, 2 * count, stride=count)
            keep = (lane >= 16 * shift) & (lane < 16 * (shift + units))
            out_ref[window, :] = jnp.where(keep, value, out_ref[window, :])
            if shift + units > 8:
                window = pl.ds(at + 1, 2 * count, stride=count)
                keep = lane < 16 * (shift + units - 8)
                out_ref[window, :] = jnp.where(keep, value, out_ref[window, :])


PLANE_MOVES = (
    (2, 2), (2, 1), (1, 2), (2, 3), (3, 2), (1, 1), (3, 3), (1, 3),
    (3, 1), (2, 0), (0, 2), (1, 0), (3, 0), (0, 1), (0, 3),
)
BATCHES = ((0, 1), (1, 2), (3, 2), (5, 2), (7, 1))


def regions_kernel(table_ref, rows_ref, out_ref, *scratch):
    held = (rows_ref,) + scratch[:7]
    stage, come, feats, shifts, plain, flipped, gram = scratch[7:14]
    ring_send, ring_recv, plane_send, plane_recv = scratch[14:]
    box, core = lax.axis_index("box"), lax.axis_index("help")
    z_at, x_at, y_at = box // PLANE, (box // 4) % 4, box % 4
    ring = (
        ((z_at + 1) % Z_SIZE * PLANE + box % PLANE, core),
        ((z_at + Z_SIZE - 1) % Z_SIZE * PLANE + box % PLANE, core),
    )

    def peer(turn):
        x_to, y_to = (x_at + turn // 8) % 4, (y_at + turn // 2 % 4) % 4
        return (z_at * PLANE + x_to * 4 + y_to, (core + turn % 2) % 2)

    barrier = pltpu.get_barrier_semaphore()
    for way in range(2):
        pl.semaphore_signal(barrier, inc=1, device_id=ring[way], device_id_type=MESH)

    def greet(turn, carry):
        pl.semaphore_signal(barrier, inc=1, device_id=peer(turn), device_id_type=MESH)
        return carry

    lax.fori_loop(1, PEERS, greet, 0)
    pl.semaphore_wait(barrier, PEERS + 1)

    def ring_copy(way, step, half):
        from_at = 0 if step == 1 else 2 * (step - 1) - 1 + way
        to_at = 7 if step == 4 else 2 * step - 1 + way
        part = pl.ds(half * (PRIM_DEV // 2), PRIM_DEV // 2)
        return pltpu.make_async_remote_copy(
            src_ref=held[from_at].at[part],
            dst_ref=held[to_at].at[part],
            send_sem=ring_send.at[way, step - 1, half],
            recv_sem=ring_recv.at[way, step - 1, half],
            device_id=ring[way],
            device_id_type=MESH,
        )

    def deal(batch):
        first, number = BATCHES[batch]

        def fill(turn, target):
            for source in range(first, first + number):
                z_from = (z_at + SOURCE_MOVES[source] + Z_SIZE) % Z_SIZE
                for slot in range(2):
                    row = table_ref[turn * 2 + slot, z_from]
                    value = held[source][jnp.maximum(row, 0)]
                    target[turn, source, slot] = jnp.where(row >= 0, value, jnp.zeros_like(value))

        def one_peer(turn):
            fill(turn, stage)
            pltpu.make_async_remote_copy(
                src_ref=stage.at[turn, pl.ds(first, number)],
                dst_ref=come.at[turn, pl.ds(first, number)],
                send_sem=plane_send.at[batch],
                recv_sem=plane_recv.at[batch],
                device_id=peer(turn),
                device_id_type=MESH,
            ).start()

        def one_core(core_move, carry):
            for x_move, y_move in PLANE_MOVES:
                one_peer(x_move * 8 + y_move * 2 + core_move)
            return carry

        lax.fori_loop(0, 2, one_core, 0)
        one_peer(1)
        fill(0, come)

    tiles = gram_tiles()
    across = (((1,), (1,)), ((), ()))

    def prepare():
        row = lax.broadcasted_iota(jnp.int32, (128, 128), 0)
        col = lax.broadcasted_iota(jnp.int32, (128, 128), 1)
        for unit in range(-7, 8):
            hit = row == col + 16 * unit
            shifts[unit + 7] = jnp.where(hit, 1.0, 0.0).astype(jnp.bfloat16)

    def collect(batch):
        first, number = BATCHES[batch]
        arrived = come.at[pl.ds(1, PEERS - 1), pl.ds(first, number)]
        pltpu.make_async_copy(arrived, arrived, plane_recv.at[batch]).wait()
        turn = turn_matrix()
        for source in range(number):

            def regroup(step, carry, source=source):
                block = come[pl.ds(step * 8, 8), first + source].reshape(256, 128)
                moved = jnp.dot(turn, block, preferred_element_type=jnp.float32)
                at = pl.multiple_of(source * 64 + step * 16, 16)
                feats[:, pl.ds(at, 16), :] = moved.astype(jnp.bfloat16).reshape(16, 16, 128)
                return carry

            lax.fori_loop(0, 4, regroup, 0, unroll=True)
        size = 64 * number
        at = (384, 0, 128, 256, 448)[batch]
        for tile, (_, _, start, width) in enumerate(tiles):
            group, skip = start // 128, start % 128 // 16
            here = feats[group, 0:size, :]
            over = lax.dot_general(
                shifts[7 - skip], here, across, preferred_element_type=jnp.float32
            )
            if skip == 0:
                down = here
            else:
                down = jnp.dot(here, shifts[7 + skip], preferred_element_type=jnp.float32)
                if skip * 16 + width > 128:
                    there = feats[group + 1, 0:size, :]
                    down += jnp.dot(there, shifts[skip - 1], preferred_element_type=jnp.float32)
                    over += lax.dot_general(
                        shifts[15 - skip], there, across, preferred_element_type=jnp.float32
                    )
            plain[tile, at : at + size, :] = down.astype(jnp.bfloat16)
            flipped[tile, :, at : at + size] = over.astype(jnp.bfloat16)

    for way in range(2):
        ring_copy(way, 1, 0).start()
    deal(0)
    for way in range(2):
        ring_copy(way, 1, 1).start()
    prepare()
    for step in range(1, 4):
        for half in range(2):
            for way in range(2):
                ring_copy(way, step, half).wait_recv()
                if step < 3 or half == way:
                    ring_copy(way, step + 1, half).start()
            if half == 0 and step > 1:
                collect(step - 2)
        deal(step)
    for way in range(2):
        ring_copy(way, 4, way).wait_recv()
    deal(4)
    for batch in range(2, 5):
        collect(batch)

    base = 0
    for m_order, (_, _, length) in enumerate(order_slices(LMAX, NBIN)):
        parts = -(-length // 128)
        for kind in range(2):
            mine = [at for at, tile in enumerate(tiles) if tile[:2] == (m_order, kind)]
            for up, up_tile in enumerate(mine):
                for over, over_tile in enumerate(mine):
                    product = jnp.dot(
                        flipped[up_tile], plain[over_tile], preferred_element_type=jnp.float32
                    )
                    at = (over, slice(up * 128, up * 128 + 128))
                    if kind == 0:
                        gram[at] = product
                    else:
                        gram[at] += product
        gram_flatten(gram, out_ref, base, length // NBIN)
        base += length * length // 128

    for step in range(1, 5):
        for half in range(2):
            for way in range(2):
                if step < 4 or half == way:
                    ring_copy(way, step, half).wait_send()
    for batch, (first, number) in enumerate(BATCHES):
        sent = stage.at[pl.ds(1, PEERS - 1), pl.ds(first, number)]
        pltpu.make_async_copy(sent, sent, plane_send.at[batch]).wait()


def region_products(table, rows):
    shape = (PEERS, Z_SIZE, 2, 16, 128)
    total = sum(length * length for _, _, length in order_slices(LMAX, NBIN))
    tiles = len(gram_tiles())
    row_total = PEERS * Z_SIZE * 2
    return pl.pallas_call(
        regions_kernel,
        out_shape=jax.ShapeDtypeStruct((total // 128, 128), jnp.float32),
        in_specs=[
            pl.BlockSpec(memory_space=pltpu.SMEM),
            pl.BlockSpec(memory_space=pltpu.VMEM),
        ],
        out_specs=pl.BlockSpec(memory_space=pltpu.VMEM),
        scratch_shapes=[pltpu.VMEM(rows.shape, rows.dtype)] * 7
        + [
            pltpu.VMEM(shape, rows.dtype),
            pltpu.VMEM(shape, rows.dtype),
            pltpu.VMEM((16, 128, 128), rows.dtype),
            pltpu.VMEM((15, 128, 128), rows.dtype),
            pltpu.VMEM((tiles, row_total, 128), rows.dtype),
            pltpu.VMEM((tiles, 128, row_total), rows.dtype),
            pltpu.VMEM((2, 256, 128), jnp.float32),
            pltpu.SemaphoreType.DMA((2, 4, 2)),
            pltpu.SemaphoreType.DMA((2, 4, 2)),
            pltpu.SemaphoreType.DMA((5,)),
            pltpu.SemaphoreType.DMA((5,)),
        ],
        compiler_params=pltpu.CompilerParams(
            collective_id=1, has_side_effects=True, vmem_limit_bytes=40 << 20
        ),
        name="region_products",
    )(table, rows)


def shards(prim_pos, prim_weight, sec_pos, sec_weight, sec_counts, tile_lists, region_of):
    pool, live, codes, spread, turn = near(
        sec_counts, sec_pos.transpose(1, 0, 2), sec_weight, region_of.reshape(1, -1)
    )
    coefficients, rows, table = pair_sums(
        tile_lists, pool, live, codes, prim_pos, prim_weight.reshape(1, -1), spread, turn
    )
    region_tensor = region_products(table, rows).reshape(1, -1)
    return (coefficients, region_tensor)


def solution(mesh):
    placed = (
        P(None, ("box", "help")),
        P(("box", "help")),
        P(("box", "help"), None, None),
        P(("box", "help"), None),
        P(("box", "help")),
        P(("box", "help"), None),
        P(("box", "help"), None),
    )
    return jax.shard_map(
        shards,
        mesh=mesh,
        in_specs=placed,
        out_specs=(P(("box", "help"), None), P(("box", "help"), None)),
        check_vma=False,
    )
```

```python
import functools
import math

import jax
import jax.numpy as jnp
from jax import lax
from jax.experimental import pallas as pl
from jax.experimental.pallas import tpu as pltpu
from jax.sharding import PartitionSpec as P

LMAX = 10
NBIN = 16
BS = 128
LIST = 12
PT = 16
PRIM_DEV = 64
NHARM = (LMAX + 1) ** 2
FEAT = NHARM * NBIN
BOXES = 128
BLK_DEV = 8
Z_SIZE = 8
PLANE = 16
SOURCE_MOVES = (0, -1, 1, -2, 2, -3, 3, 4)
PEERS = 2 * PLANE
MESH = pl.DeviceIdType.MESH

GROUPS = ((0, 1, 2, 3, 4, 5, 6, 7, 8, 9, 10),)


def order_slices(degree_top, bin_count):
    slices = []
    position = 0
    for m_order in range(degree_top + 1):
        length = (degree_top + 1 - m_order) * bin_count
        if m_order == 0:
            slices.append((position, -1, length))
            position = position + length
        else:
            slices.append((position, position + length, length))
            position = position + 2 * length
    return slices


def harmonic_scale(m_order, degree):
    factor = math.sqrt(
        (2 * degree + 1)
        / (4.0 * math.pi)
        * math.factorial(degree - m_order)
        / math.factorial(degree + m_order)
    )
    if m_order > 0:
        factor = factor * math.sqrt(2.0)
    lead = 1.0
    for odd_value in range(1, 2 * m_order, 2):
        lead = lead * odd_value
    for step in range(m_order + 1, degree + 1):
        lead = lead * (2 * step - 1) / (step - m_order)
    return factor * lead


def harmonic_scales():
    scales = []
    for m_order in range(LMAX + 1):
        row = [harmonic_scale(m_order, degree) for degree in range(m_order, LMAX + 1)]
        scales += row if m_order == 0 else row + row
    return scales


def first_row(m_order):
    return order_slices(LMAX, 1)[m_order][0]


def turn_matrix():
    row = lax.broadcasted_iota(jnp.int32, (256, 256), 0)
    col = lax.broadcasted_iota(jnp.int32, (256, 256), 1)
    return jnp.where(col == (row % 16) * 16 + row // 16, 1.0, 0.0).astype(jnp.bfloat16)


def near_kernel(
    counts_ref, pos_ref, weight_ref, region_ref,
    pool_ref, live_ref, code_ref, spread_ref, turn_ref, send, recv
):
    box, core = lax.axis_index("box"), lax.axis_index("help")
    z_at, other = box // PLANE, 1 - core
    above, below = (box + 1) % BOXES, (box + BOXES - 1) % BOXES
    near = ((above, 0, 0), (above, 1, 0), (below, 0, 2), (below, 1, 2), (box, other, 1))
    line = [((z_at + step) % Z_SIZE * PLANE + box % PLANE, core) for step in range(1, Z_SIZE)]
    barrier = pltpu.get_barrier_semaphore()
    for to_box, to_core, _ in near:
        pl.semaphore_signal(barrier, inc=1, device_id=(to_box, to_core), device_id_type=MESH)
    for target in line:
        pl.semaphore_signal(barrier, inc=1, device_id=target, device_id_type=MESH)

    lane = lax.broadcasted_iota(jnp.int32, (1, BS), 1)
    mine = 2 + core
    live = jnp.zeros((1, BS), jnp.int32)
    for block in range(BLK_DEV):
        count = counts_ref[block]
        live = jnp.where(lane == block, count, live)
        for axis in range(3):
            pool_ref[mine, block, axis : axis + 1, :] = pos_ref[axis, block : block + 1, :]
        pool_ref[mine, block, 3:4, :] = jnp.where(lane < count, weight_ref[block : block + 1, :], 0.0)
    live_ref[mine] = live
    row = lax.broadcasted_iota(jnp.int32, (PRIM_DEV, BS), 0)
    col = lax.broadcasted_iota(jnp.int32, (PRIM_DEV, BS), 1)
    over = jnp.concatenate([region_ref[...], jnp.zeros((1, BS - PRIM_DEV), jnp.int32)], axis=1)
    down = jnp.sum(jnp.where(row == col, over, 0), axis=1, keepdims=True)
    rank = jnp.sum(jnp.where((down == over) & (row < col), 1, 0), axis=0, keepdims=True)
    code_ref[z_at] = jnp.where(lane < PRIM_DEV, 2 * over + rank, -1)

    pl.semaphore_wait(barrier, 12)

    def push(kind, ref, from_at, to_at, target):
        pltpu.make_async_remote_copy(
            src_ref=ref.at[from_at],
            dst_ref=ref.at[to_at],
            send_sem=send.at[kind],
            recv_sem=recv.at[kind],
            device_id=target,
            device_id_type=MESH,
        ).start()

    for step in (4, 3, 5, 2, 6, 1, 7):
        push(2, code_ref, z_at, z_at, line[step - 1])
    for to_box, to_core, move in near:
        push(0, pool_ref, mine, 2 * move + core, (to_box, to_core))
        push(1, live_ref, mine, 2 * move + core, (to_box, to_core))
    row = lax.broadcasted_iota(jnp.int32, (128, 128), 0)
    col = lax.broadcasted_iota(jnp.int32, (128, 128), 1)
    for part in range(8):
        hit = col - part * NBIN == row // 8
        spread_ref[part] = jnp.where(hit, 1.0, 0.0).astype(jnp.bfloat16)
    turn_ref[...] = turn_matrix()
    for sems in (recv, send):
        for kind, (ref, number) in enumerate(((pool_ref, 5), (live_ref, 5), (code_ref, 7))):
            moved = ref.at[pl.ds(0, number)]
            pltpu.make_async_copy(moved, moved, sems.at[kind]).wait()


def near(counts, pos, weight, regions):
    return pl.pallas_call(
        near_kernel,
        out_shape=(
            jax.ShapeDtypeStruct((6, BLK_DEV, 4, BS), jnp.float32),
            jax.ShapeDtypeStruct((6, 1, BS), jnp.int32),
            jax.ShapeDtypeStruct((Z_SIZE, 1, BS), jnp.int32),
            jax.ShapeDtypeStruct((8, 128, 128), jnp.bfloat16),
            jax.ShapeDtypeStruct((256, 256), jnp.bfloat16),
        ),
        in_specs=[pl.BlockSpec(memory_space=pltpu.SMEM)]
        + [pl.BlockSpec(memory_space=pltpu.VMEM)] * 3,
        out_specs=(pl.BlockSpec(memory_space=pltpu.VMEM),) * 5,
        scratch_shapes=[pltpu.SemaphoreType.DMA((3,)), pltpu.SemaphoreType.DMA((3,))],
        compiler_params=pltpu.CompilerParams(
            collective_id=0, has_side_effects=True, vmem_limit_bytes=8 << 20
        ),
        name="near",
    )(counts, pos, weight, regions)


def pair_kernel(
    list_ref, pool_ref, live_ref, code_ref, pos_ref, weight_ref, spread, turn_ref,
    coef_ref, rows_ref, table_ref, packed, basis, spline, acc, diag, live, sem
):
    tile = pl.program_id(0)
    box, core = lax.axis_index("box"), lax.axis_index("help")
    lane = lax.broadcasted_iota(jnp.int32, (4, BS), 1)

    @pl.when(tile == 0)
    def _():
        fetch = pltpu.make_async_copy(live_ref, live, sem)
        fetch.start()
        turn = lax.broadcasted_iota(jnp.int32, (2 * PEERS, BS), 0)
        over = lax.broadcasted_iota(jnp.int32, (2 * PEERS, BS), 1)
        x_to, y_to = (box // 4 + turn // 16) % 4, (box + turn // 4) % 4
        owner = (box // PLANE * PLANE + x_to * 4 + y_to) * 2 + (core + turn // 2) % 2
        wanted = owner * 2 + turn % 2
        table = jnp.zeros((2 * PEERS, BS), jnp.int32)
        for z_from in range(Z_SIZE):
            found = jnp.max(
                jnp.where(code_ref[z_from] == wanted, over, -1), axis=1, keepdims=True
            )
            table = jnp.where(over == z_from, found, table)
        table_ref[...] = table
        fetch.wait()

    packed[...] = jnp.zeros_like(packed)
    filled = jnp.int32(0)
    for slot in range(LIST):
        listed = list_ref[tile, slot]
        used = listed >= 0
        listed = jnp.maximum(listed, 0)
        owner, inner = listed >> 3, listed & (BLK_DEV - 1)
        place = jnp.where(used, (((owner >> 1) - box + 1) & (BOXES - 1)) * 2 + (owner & 1), 0)
        block = pool_ref[place, inner]
        base = filled >> 7
        shift = filled & (BS - 1)
        moved = pltpu.roll(block, shift, 1)
        low = jnp.where((lane >= shift) & used, moved, packed[base])
        packed[base] = low
        high = jnp.where((lane < shift) & used, moved, packed[base + 1])
        packed[base + 1] = high
        filled = filled + jnp.where(used, live[place, 0, inner], 0)
    chunks = (filled + 2 * BS - 1) >> 8

    acc[...] = jnp.zeros_like(acc)
    own = lax.broadcasted_iota(jnp.int32, (PT, PRIM_DEV), 0) + tile * PT
    own = own == lax.broadcasted_iota(jnp.int32, (PT, PRIM_DEV), 1)

    def column(values):
        return jnp.sum(jnp.where(own, values, 0.0), axis=1, keepdims=True)

    px, py, pz = [column(pos_ref[axis : axis + 1, :]) for axis in range(3)]
    scale_column = column(weight_ref[...]) * (1.0 / math.sqrt(LIST * BS))
    bin_step = 1.0 / (NBIN + 1)

    def chunk_step(chunk, carry):
        geometry = []
        for half in range(2):
            rows = packed[2 * chunk + half]
            dx = rows[0:1, :] - px
            dy = rows[1:2, :] - py
            dz = rows[2:3, :] - pz
            weight = jnp.broadcast_to(rows[3:4, :], (PT, BS))
            radius = jnp.sqrt(dx * dx + dy * dy + dz * dz)
            inverse = 1.0 / jnp.maximum(radius, 0.5 * bin_step)
            geometry.append((dx * inverse, dy * inverse, dz * inverse))
            place = radius * float(NBIN + 1)
            whole = jnp.floor(place)
            part = place - whole
            upper = weight * part
            lower = weight * (1.0 - part)
            cols = slice(half * BS, (half + 1) * BS)
            above = jnp.where(whole == 0.0, upper, 0.0)
            hats = []
            for bin_at in range(NBIN):
                here = whole == float(bin_at + 1)
                hats.append(jnp.where(here, lower, above))
                above = jnp.where(here, upper, 0.0)
            for side in range(2):
                part_rows = slice(side * 8, side * 8 + 8)
                for bin_at in range(0, NBIN, 2):
                    both = jnp.concatenate([hats[bin_at][part_rows], hats[bin_at + 1][part_rows]])
                    at = side * 128 + bin_at * 8
                    spline[at : at + 16, cols] = both.astype(jnp.bfloat16)
        angular = [[None, None], [None, None]]
        for orders in GROUPS:
            for half in range(2):
                ux, uy, uz = geometry[half]
                cols = slice(half * BS, (half + 1) * BS)
                for m_order in orders:
                    if m_order == 1:
                        angular[half] = [ux, uy]
                    elif m_order > 1:
                        cos_part, sin_part = angular[half]
                        angular[half] = [
                            cos_part * ux - sin_part * uy,
                            sin_part * ux + cos_part * uy,
                        ]
                    older, newer = None, None
                    start = first_row(m_order)
                    count = LMAX + 1 - m_order
                    for degree in range(m_order, LMAX + 1):
                        if degree == m_order:
                            current = None
                        elif degree == m_order + 1:
                            current = uz
                        else:
                            ratio = (degree + m_order - 1) * (degree - m_order - 1) / (
                                (2 * degree - 1) * (2 * degree - 3)
                            )
                            if older is None:
                                current = uz * newer - ratio
                            else:
                                current = uz * newer - ratio * older
                        older, newer = newer, current
                        at = (start + degree - m_order) * PT
                        if m_order == 0:
                            value = jnp.ones((PT, BS), jnp.float32) if current is None else current
                            basis[at : at + PT, cols] = value.astype(jnp.bfloat16)
                        else:
                            for kind in range(2):
                                turn = angular[half][kind]
                                value = turn if current is None else current * turn
                                low = at + kind * count * PT
                                basis[low : low + PT, cols] = value.astype(jnp.bfloat16)
            first = first_row(orders[0]) * PT
            last = NHARM * PT if orders[-1] == LMAX else first_row(orders[-1] + 1) * PT
            product = lax.dot_general(
                basis[first:last, :],
                spline[...],
                (((1,), (1,)), ((), ())),
                preferred_element_type=jnp.float32,
            ).reshape(-1, 2, 8, 2 * BS)
            wanted = jnp.concatenate(
                [product[:, 0:1, :, 0:128], product[:, 1:2, :, 128:256]], axis=1
            )
            acc[first:last, :] += wanted.reshape(last - first, 128)
        return carry

    lax.fori_loop(0, chunks, chunk_step, 0)

    row = lax.broadcasted_iota(jnp.int32, (PT, 128), 0)
    col = lax.broadcasted_iota(jnp.int32, (PT, 128), 1)
    keep = jnp.where((col & 7) == (row & 7), scale_column, 0.0)
    scales = harmonic_scales()
    for harm in range(128):
        if harm < NHARM:
            value = acc[harm * PT : (harm + 1) * PT, :] * (keep * scales[harm])
            value = value.astype(jnp.bfloat16)
        else:
            value = jnp.zeros((PT, 128), jnp.bfloat16)
        diag[harm % 8, (harm // 8) * PT : (harm // 8 + 1) * PT, :] = value
    total = jnp.zeros((256, 128), jnp.float32)
    for part in range(8):
        total = total + jnp.dot(diag[part], spread[part], preferred_element_type=jnp.float32)
    rows = total.astype(jnp.bfloat16)
    for group in range(15):
        coef_ref[:, group * 128 : (group + 1) * 128] = rows[group * PT : (group + 1) * PT, :]
    coef_ref[:, 1920:FEAT] = rows[15 * PT : 16 * PT, : FEAT - 1920]
    turned = jnp.dot(turn_ref[...], rows, preferred_element_type=jnp.float32)
    rows_ref[...] = turned.astype(jnp.bfloat16).reshape(PT, 16, 128)


def pair_sums(lists, *operands):
    tiles = lists.shape[0]
    live = operands[1]
    return pl.pallas_call(
        pair_kernel,
        out_shape=(
            jax.ShapeDtypeStruct((tiles * PT, FEAT), jnp.bfloat16),
            jax.ShapeDtypeStruct((tiles * PT, 16, 128), jnp.bfloat16),
            jax.ShapeDtypeStruct((2 * PEERS, BS), jnp.int32),
        ),
        grid_spec=pltpu.PrefetchScalarGridSpec(
            num_scalar_prefetch=1,
            grid=(tiles,),
            in_specs=[pl.BlockSpec(memory_space=pltpu.VMEM)] * len(operands),
            out_specs=(
                pl.BlockSpec((PT, FEAT), lambda t, *_: (t, 0)),
                pl.BlockSpec((PT, 16, 128), lambda t, *_: (t, 0, 0)),
                pl.BlockSpec((2 * PEERS, BS), lambda t, *_: (0, 0)),
            ),
            scratch_shapes=[
                pltpu.VMEM((2 * ((LIST + 1) // 2) + 2, 4, BS), jnp.float32),
                pltpu.VMEM((NHARM * PT, 2 * BS), jnp.bfloat16),
                pltpu.VMEM((NBIN * PT, 2 * BS), jnp.bfloat16),
                pltpu.VMEM((NHARM * PT, 128), jnp.float32),
                pltpu.VMEM((8, 256, 128), jnp.bfloat16),
                pltpu.SMEM(live.shape, live.dtype),
                pltpu.SemaphoreType.DMA(()),
            ],
        ),
        compiler_params=pltpu.CompilerParams(vmem_limit_bytes=40 << 20),
        name="pair_sums",
    )(lists, *operands)


def gram_tiles():
    tiles = []
    for m_order, (cos_start, sin_start, length) in enumerate(order_slices(LMAX, NBIN)):
        for kind, start in enumerate((cos_start, sin_start)):
            if start >= 0:
                for part in range(-(-length // 128)):
                    width = min(128, length - 128 * part)
                    tiles.append((m_order, kind, start + 128 * part, width))
    return tiles


def gram_flatten(gram, out_ref, base, count):
    lane = lax.broadcasted_iota(jnp.int32, (2 * count, 128), 1)
    for rest in range(8):
        for part in range(-(-count // 8)):
            units = min(8, count - 8 * part)
            shift = rest * count % 8
            at = base + rest * count // 8 + part
            value = gram[part, pl.ds(rest, 2 * count, stride=8), :] * (1.0 / PRIM_DEV)
            if shift:
                value = pltpu.roll(value, 16 * shift, 1)
            window = pl.ds(at, 2 * count, stride=count)
            keep = (lane >= 16 * shift) & (lane < 16 * (shift + units))
            out_ref[window, :] = jnp.where(keep, value, out_ref[window, :])
            if shift + units > 8:
                window = pl.ds(at + 1, 2 * count, stride=count)
                keep = lane < 16 * (shift + units - 8)
                out_ref[window, :] = jnp.where(keep, value, out_ref[window, :])


PLANE_MOVES = (
    (2, 2), (2, 1), (1, 2), (2, 3), (3, 2), (1, 1), (3, 3), (1, 3),
    (3, 1), (2, 0), (0, 2), (1, 0), (3, 0), (0, 1), (0, 3),
)
BATCHES = ((0, 1), (1, 2), (3, 2), (5, 2), (7, 1))


def regions_kernel(table_ref, rows_ref, out_ref, *scratch):
    held = (rows_ref,) + scratch[:7]
    stage, come, feats, shifts, plain, flipped, gram = scratch[7:14]
    ring_send, ring_recv, plane_send, plane_recv = scratch[14:]
    box, core = lax.axis_index("box"), lax.axis_index("help")
    z_at, x_at, y_at = box // PLANE, (box // 4) % 4, box % 4
    ring = (
        ((z_at + 1) % Z_SIZE * PLANE + box % PLANE, core),
        ((z_at + Z_SIZE - 1) % Z_SIZE * PLANE + box % PLANE, core),
    )

    def peer(turn):
        x_to, y_to = (x_at + turn // 8) % 4, (y_at + turn // 2 % 4) % 4
        return (z_at * PLANE + x_to * 4 + y_to, (core + turn % 2) % 2)

    barrier = pltpu.get_barrier_semaphore()
    for way in range(2):
        pl.semaphore_signal(barrier, inc=1, device_id=ring[way], device_id_type=MESH)

    def greet(turn, carry):
        pl.semaphore_signal(barrier, inc=1, device_id=peer(turn), device_id_type=MESH)
        return carry

    lax.fori_loop(1, PEERS, greet, 0)
    pl.semaphore_wait(barrier, PEERS + 1)

    def ring_copy(way, step, half):
        from_at = 0 if step == 1 else 2 * (step - 1) - 1 + way
        to_at = 7 if step == 4 else 2 * step - 1 + way
        part = pl.ds(half * (PRIM_DEV // 2), PRIM_DEV // 2)
        return pltpu.make_async_remote_copy(
            src_ref=held[from_at].at[part],
            dst_ref=held[to_at].at[part],
            send_sem=ring_send.at[way, step - 1, half],
            recv_sem=ring_recv.at[way, step - 1, half],
            device_id=ring[way],
            device_id_type=MESH,
        )

    def deal(batch):
        first, number = BATCHES[batch]

        def fill(turn, target):
            for source in range(first, first + number):
                z_from = (z_at + SOURCE_MOVES[source] + Z_SIZE) % Z_SIZE
                for slot in range(2):
                    row = table_ref[turn * 2 + slot, z_from]
                    value = held[source][jnp.maximum(row, 0)]
                    target[turn, source, slot] = jnp.where(row >= 0, value, jnp.zeros_like(value))

        def one_peer(turn):
            fill(turn, stage)
            pltpu.make_async_remote_copy(
                src_ref=stage.at[turn, pl.ds(first, number)],
                dst_ref=come.at[turn, pl.ds(first, number)],
                send_sem=plane_send.at[batch],
                recv_sem=plane_recv.at[batch],
                device_id=peer(turn),
                device_id_type=MESH,
            ).start()

        def one_core(core_move, carry):
            for x_move, y_move in PLANE_MOVES:
                one_peer(x_move * 8 + y_move * 2 + core_move)
            return carry

        lax.fori_loop(0, 2, one_core, 0)
        one_peer(1)
        fill(0, come)

    tiles = gram_tiles()
    across = (((1,), (1,)), ((), ()))

    def prepare():
        row = lax.broadcasted_iota(jnp.int32, (128, 128), 0)
        col = lax.broadcasted_iota(jnp.int32, (128, 128), 1)
        for unit in range(-7, 8):
            hit = row == col + 16 * unit
            shifts[unit + 7] = jnp.where(hit, 1.0, 0.0).astype(jnp.bfloat16)

    def collect(batch):
        first, number = BATCHES[batch]
        arrived = come.at[pl.ds(1, PEERS - 1), pl.ds(first, number)]
        pltpu.make_async_copy(arrived, arrived, plane_recv.at[batch]).wait()
        turn = turn_matrix()
        for source in range(number):

            def regroup(step, carry, source=source):
                block = come[pl.ds(step * 8, 8), first + source].reshape(256, 128)
                moved = jnp.dot(turn, block, preferred_element_type=jnp.float32)
                at = pl.multiple_of(source * 64 + step * 16, 16)
                feats[:, pl.ds(at, 16), :] = moved.astype(jnp.bfloat16).reshape(16, 16, 128)
                return carry

            lax.fori_loop(0, 4, regroup, 0, unroll=True)
        size = 64 * number
        at = (384, 0, 128, 256, 448)[batch]
        for tile, (_, _, start, width) in enumerate(tiles):
            group, skip = start // 128, start % 128 // 16
            here = feats[group, 0:size, :]
            over = lax.dot_general(
                shifts[7 - skip], here, across, preferred_element_type=jnp.float32
            )
            if skip == 0:
                down = here
            else:
                down = jnp.dot(here, shifts[7 + skip], preferred_element_type=jnp.float32)
                if skip * 16 + width > 128:
                    there = feats[group + 1, 0:size, :]
                    down += jnp.dot(there, shifts[skip - 1], preferred_element_type=jnp.float32)
                    over += lax.dot_general(
                        shifts[15 - skip], there, across, preferred_element_type=jnp.float32
                    )
            plain[tile, at : at + size, :] = down.astype(jnp.bfloat16)
            flipped[tile, :, at : at + size] = over.astype(jnp.bfloat16)

    for way in range(2):
        ring_copy(way, 1, 0).start()
    deal(0)
    for way in range(2):
        ring_copy(way, 1, 1).start()
    prepare()
    for step in range(1, 4):
        for half in range(2):
            for way in range(2):
                ring_copy(way, step, half).wait_recv()
                if step < 3 or half == way:
                    ring_copy(way, step + 1, half).start()
            if half == 0 and step > 1:
                collect(step - 2)
        deal(step)
    for way in range(2):
        ring_copy(way, 4, way).wait_recv()
    deal(4)
    for batch in range(2, 5):
        collect(batch)

    base = 0
    for m_order, (_, _, length) in enumerate(order_slices(LMAX, NBIN)):
        parts = -(-length // 128)
        for kind in range(2):
            mine = [at for at, tile in enumerate(tiles) if tile[:2] == (m_order, kind)]
            for up, up_tile in enumerate(mine):
                for over, over_tile in enumerate(mine):
                    product = jnp.dot(
                        flipped[up_tile], plain[over_tile], preferred_element_type=jnp.float32
                    )
                    at = (over, slice(up * 128, up * 128 + 128))
                    if kind == 0:
                        gram[at] = product
                    else:
                        gram[at] += product
        gram_flatten(gram, out_ref, base, length // NBIN)
        base += length * length // 128

    for step in range(1, 5):
        for half in range(2):
            for way in range(2):
                if step < 4 or half == way:
                    ring_copy(way, step, half).wait_send()
    for batch, (first, number) in enumerate(BATCHES):
        sent = stage.at[pl.ds(1, PEERS - 1), pl.ds(first, number)]
        pltpu.make_async_copy(sent, sent, plane_send.at[batch]).wait()


def region_products(table, rows):
    shape = (PEERS, Z_SIZE, 2, 16, 128)
    total = sum(length * length for _, _, length in order_slices(LMAX, NBIN))
    tiles = len(gram_tiles())
    row_total = PEERS * Z_SIZE * 2
    return pl.pallas_call(
        regions_kernel,
        out_shape=jax.ShapeDtypeStruct((total // 128, 128), jnp.float32),
        in_specs=[
            pl.BlockSpec(memory_space=pltpu.SMEM),
            pl.BlockSpec(memory_space=pltpu.VMEM),
        ],
        out_specs=pl.BlockSpec(memory_space=pltpu.VMEM),
        scratch_shapes=[pltpu.VMEM(rows.shape, rows.dtype)] * 7
        + [
            pltpu.VMEM(shape, rows.dtype),
            pltpu.VMEM(shape, rows.dtype),
            pltpu.VMEM((16, 128, 128), rows.dtype),
            pltpu.VMEM((15, 128, 128), rows.dtype),
            pltpu.VMEM((tiles, row_total, 128), rows.dtype),
            pltpu.VMEM((tiles, 128, row_total), rows.dtype),
            pltpu.VMEM((2, 256, 128), jnp.float32),
            pltpu.SemaphoreType.DMA((2, 4, 2)),
            pltpu.SemaphoreType.DMA((2, 4, 2)),
            pltpu.SemaphoreType.DMA((5,)),
            pltpu.SemaphoreType.DMA((5,)),
        ],
        compiler_params=pltpu.CompilerParams(
            collective_id=1, has_side_effects=True, vmem_limit_bytes=40 << 20
        ),
        name="region_products",
    )(table, rows)


def shards(prim_pos, prim_weight, sec_pos, sec_weight, sec_counts, tile_lists, region_of):
    pool, live, codes, spread, turn = near(
        sec_counts, sec_pos.transpose(1, 0, 2), sec_weight, region_of.reshape(1, -1)
    )
    coefficients, rows, table = pair_sums(
        tile_lists, pool, live, codes, prim_pos, prim_weight.reshape(1, -1), spread, turn
    )
    region_tensor = region_products(table, rows).reshape(1, -1)
    return (coefficients, region_tensor)


def solution(mesh):
    placed = (
        P(None, ("box", "help")),
        P(("box", "help")),
        P(("box", "help"), None, None),
        P(("box", "help"), None),
        P(("box", "help")),
        P(("box", "help"), None),
        P(("box", "help"), None),
    )
    return jax.shard_map(
        shards,
        mesh=mesh,
        in_specs=placed,
        out_specs=(P(("box", "help"), None), P(("box", "help"), None)),
        check_vma=False,
    )
```
